256 devices in a mesh: dp: 8 (over z), ctx: 32 (over x, y, core).
Axes of the slice: x: 4, y: 4, z: 8, core: 2. Of those that a mesh axis runs over, the one named last changes fastest.
Arguments:
- queries: bfloat16 [8, 4096, 4096], P('dp', 'ctx'), may hold values from -120 to 120
- layer_input: bfloat16 [8, 4096, 4096], P('dp', 'ctx'), may hold values from -6 to 6
- key_value_weight: bfloat16 [4096, 1024], P(('dp', 'ctx')), may hold values from -0.25 to 0.25
- output_gradient: bfloat16 [8, 4096, 4096], P('dp', 'ctx'), may hold values from -6 to 6
- document_lengths: int32 [8, 32], P('dp'), may hold values from 1 to 1024, 4096 in all within a row
Outputs:
- attended: bfloat16 [8, 4096, 4096], P('dp', 'ctx')
- query_grad: bfloat16 [8, 4096, 4096], P('dp', 'ctx')
- input_grad: bfloat16 [8, 4096, 4096], P('dp', 'ctx')
The draws below stay inside these ranges and needn't reach their ends.
Inputs may be any that keep to these rules, and one draw needn't show every extreme that they name: `document_lengths`: each row holds the lengths of the 32 documents of one sequence in order; they sum to 4096, and one of them is exactly 1024.
All inputs are finite; a program needn't handle non-finite values.
Results may differ from the reference program's by a relative error of at most 0.02.
The reference program's roundings to bfloat16 on the way count: a program that leaves them out, or rounds other values in their place, can miss the bound.
Values may be sent and summed in bfloat16 or wider, within the bound.
A program may use at most 128 MiB of HBM per device.

```python
import math
import jax
import jax.numpy as jnp
import numpy as np
from jax import lax

D = 4096
QUERY_HEADS = 32
KEY_VALUE_HEADS = 4
HEAD_SIZE = 128
TOK_DEV = 128
SEQUENCE_TOKENS = 4096
MAXDOC = 1024
NDOC = 32
KVW = 1024
N_DP = 8
N_CTX = 32


def draw_queries(key, part):
    first_key = jax.random.fold_in(key, 11)
    shape = (N_DP, SEQUENCE_TOKENS, QUERY_HEADS * HEAD_SIZE)
    value_rows = jnp.clip(jax.random.normal(first_key, shape, jnp.float32), -6.0, 6.0)
    return value_rows.astype(jnp.bfloat16)


def steps_of(key, shape, pieces, least, high):
    level, own = 1.0, jax.random.fold_in(key, 6)
    for position, blocks in pieces:
        heights = jnp.exp(jax.random.uniform(jax.random.fold_in(own, position), (blocks,), jnp.float32, least / len(pieces), high / len(pieces)))
        level = level * jnp.repeat(heights, shape[position] // blocks).reshape([-1 if axis == position else 1 for axis in range(len(shape))])
    return level


def length_profile(count, total, reach, skew):
    weights = [(1 << 20) // math.isqrt(grade ** skew) + 1 for grade in range(2, count + 1)]
    surplus, holding = total - reach - (count - 1), [1] * (count - 1)
    while surplus > 0:
        free = [i for i in range(count - 1) if holding[i] < reach]
        whole, budget = sum([weights[i] for i in free]), surplus
        for i in free:
            extra = min(reach - holding[i], max(1, budget * weights[i] // whole), surplus)
            holding[i] = holding[i] + extra
            surplus = surplus - extra
    return np.array([reach] + holding)


def uneven(rng, count, total, most, lean):
    if count == 2:
        one = jax.random.randint(rng, (), max(1, total - most), min(most, total - 1) + 1)
        return jnp.stack([one, total - one])
    tallies = jnp.asarray(length_profile(count, total, most, lean), jnp.int32)
    pairs = (count - 1) // 2
    giver, taker = tallies[1:1 + 2 * pairs:2], tallies[2:2 + 2 * pairs:2]
    slack = jnp.minimum(giver - 1, most - taker)
    passed = jax.random.randint(jax.random.fold_in(rng, 1), (pairs,), 0, 1 << 20) % (slack + 1)
    tallies = tallies.at[1:1 + 2 * pairs:2].set(giver - passed).at[2:2 + 2 * pairs:2].set(taker + passed)
    return tallies[jax.random.permutation(jax.random.fold_in(rng, 2), count)]


def scatter_about(key, dims, scale, most, pieces=(), held_as=jnp.bfloat16):
    values = scale * jax.random.normal(key, dims, jnp.float32)
    if pieces:
        values = values * steps_of(key, dims, pieces, -0.22, 0.18)
    return jnp.clip(values, -most, most).astype(held_as)


def setup_inputs(seed: int = 0) -> dict:
    splits = jax.random.split(jax.random.key(seed), 6)
    return {
        "queries": draw_queries(jax.random.fold_in(splits[5], 71), 0),
        "layer_input": scatter_about(splits[1], (N_DP, SEQUENCE_TOKENS, D), 1.0, 6.0, ((0, 8), (1, 32))),
        "key_value_weight": scatter_about(splits[2], (D, KVW), (KVW // 2) ** -0.5, 0.25, ((0, 256),)),
        "output_gradient": scatter_about(splits[3], (N_DP, SEQUENCE_TOKENS, QUERY_HEADS * HEAD_SIZE), 1.0, 6.0, ((0, 8), (1, 32))),
        "document_lengths": jax.vmap(lambda own: uneven(own, NDOC, SEQUENCE_TOKENS, MAXDOC, 2))(jax.random.split(splits[4], N_DP)).reshape((N_DP, NDOC)).astype(jnp.int32),
    }


masked_score = -1e+30

def document_of(positions, ends):
    return lax.optimization_barrier(jnp.sum((positions[..., None] >= ends).astype(jnp.int32), axis=-1))

def reference(queries, layer_input, key_value_weight, output_gradient, document_lengths):
    head_group = QUERY_HEADS // KEY_VALUE_HEADS
    window_reach = N_CTX // 4
    block_slice = TOK_DEV
    window = (window_reach + 1) * block_slice
    half_length = KEY_VALUE_HEADS * HEAD_SIZE
    scale = 1.0 / math.sqrt(HEAD_SIZE)

    def one_sequence(items):
        query_sequence, input_seq, gradient_sequence, lengths = items
        ends = jnp.cumsum(lengths).astype(jnp.int32)
        projected_input = jnp.dot(input_seq, key_value_weight, preferred_element_type=jnp.float32).astype(jnp.bfloat16)
        pad_tokens = jnp.zeros((window_reach * block_slice, KEY_VALUE_HEADS, HEAD_SIZE), jnp.bfloat16)
        key_rows = jnp.concatenate([pad_tokens, projected_input[:, :half_length].reshape(SEQUENCE_TOKENS, KEY_VALUE_HEADS, HEAD_SIZE)], axis=0)
        value_rows = jnp.concatenate([pad_tokens, projected_input[:, half_length:].reshape(SEQUENCE_TOKENS, KEY_VALUE_HEADS, HEAD_SIZE)], axis=0)

        def advance(buffer, index):
            leading = index * block_slice
            query_tile_block = lax.dynamic_slice_in_dim(query_sequence, leading, block_slice, 0).reshape(block_slice, KEY_VALUE_HEADS, head_group, HEAD_SIZE).astype(jnp.float32)
            gradient_block = lax.dynamic_slice_in_dim(gradient_sequence, leading, block_slice, 0).reshape(block_slice, KEY_VALUE_HEADS, head_group, HEAD_SIZE).astype(jnp.float32)
            key_block = lax.dynamic_slice_in_dim(key_rows, leading, window, 0).astype(jnp.float32)
            value_block = lax.dynamic_slice_in_dim(value_rows, leading, window, 0).astype(jnp.float32)
            query_pos = leading + jnp.arange(block_slice, dtype=jnp.int32)
            key_pos = leading - window_reach * block_slice + jnp.arange(window, dtype=jnp.int32)
            allowed = (document_of(query_pos, ends)[:, None] == document_of(key_pos, ends)[None, :]) & (key_pos[None, :] <= query_pos[:, None]) & (key_pos[None, :] >= 0)
            score = scale * jnp.einsum('qhgd,khd->hgqk', query_tile_block, key_block)
            top = lax.optimization_barrier(jnp.max(jnp.where(allowed, score, masked_score), axis=-1))
            weight = jnp.exp(jnp.where(allowed, score - top[..., None], masked_score))
            total = lax.optimization_barrier(jnp.sum(weight, axis=-1))
            mixed = jnp.einsum('hgqk,khd->qhgd', weight.astype(jnp.bfloat16).astype(jnp.float32), value_block)
            output = (mixed / jnp.transpose(total, (2, 0, 1))[..., None]).astype(jnp.bfloat16)
            logsum = top + jnp.log(total)
            product = jnp.transpose(lax.optimization_barrier(jnp.sum(gradient_block * output.astype(jnp.float32), axis=-1)), (1, 2, 0))
            prob = jnp.exp(jnp.where(allowed, score - logsum[..., None], masked_score))
            pressure = jnp.einsum('qhgd,khd->hgqk', gradient_block, value_block)
            slope = (prob * (pressure - product[..., None])).astype(jnp.bfloat16).astype(jnp.float32)
            query_sum = scale * jnp.einsum('hgqk,khd->qhgd', slope, key_block)
            key_part = scale * jnp.einsum('hgqk,qhgd->khd', slope, query_tile_block)
            value_part = jnp.einsum('hgqk,qhgd->khd', prob.astype(jnp.bfloat16).astype(jnp.float32), gradient_block)
            piece = jnp.concatenate([key_part, value_part], axis=-1)
            buffer = lax.dynamic_update_slice_in_dim(buffer, lax.dynamic_slice_in_dim(buffer, leading, window, 0) + piece, leading, 0)
            return (buffer, (output.reshape(block_slice, QUERY_HEADS * HEAD_SIZE), query_sum.astype(jnp.bfloat16).reshape(block_slice, QUERY_HEADS * HEAD_SIZE)))
        start_store = jnp.zeros((SEQUENCE_TOKENS + window_reach * block_slice, KEY_VALUE_HEADS, 2 * HEAD_SIZE), jnp.float32)
        buffer, (outputs, sums) = lax.scan(advance, start_store, jnp.arange(SEQUENCE_TOKENS // block_slice, dtype=jnp.int32))
        outputs = outputs.reshape(SEQUENCE_TOKENS, QUERY_HEADS * HEAD_SIZE)
        sums = sums.reshape(SEQUENCE_TOKENS, QUERY_HEADS * HEAD_SIZE)
        gradient_value = buffer[window_reach * block_slice:].astype(jnp.bfloat16)
        flat = jnp.concatenate([gradient_value[..., :HEAD_SIZE].reshape(SEQUENCE_TOKENS, half_length), gradient_value[..., HEAD_SIZE:].reshape(SEQUENCE_TOKENS, half_length)], axis=1)
        input_grad = jnp.dot(flat, key_value_weight.T, preferred_element_type=jnp.float32).astype(jnp.bfloat16)
        return (outputs, sums, input_grad)
    attended, query_grad, input_grad = lax.map(one_sequence, (queries, layer_input, output_gradient, document_lengths))
    return (attended, query_grad, input_grad)
```

```python
import functools
import math

import jax
import jax.numpy as jnp
from jax import lax
from jax.experimental import pallas as pl
from jax.experimental.pallas import tpu as pltpu
from jax.sharding import PartitionSpec as P

QUERY_HEADS = 32
KEY_VALUE_HEADS = 4
HEAD_SIZE = 128
GROUP = QUERY_HEADS // KEY_VALUE_HEADS
NX, NY, NZ = 4, 4, 8
TOKENS = 128
PAIR = 2 * TOKENS
MODEL = 4096
HALF = MODEL // 2
SCALE = 1.0 / math.sqrt(HEAD_SIZE)
LOG2E = math.log2(math.e)
MESH = pl.DeviceIdType.MESH
F32 = jnp.float32
BF16 = jnp.bfloat16

PARTS = (
    (0, 0, 0, 32, "zyx"),
    (0, 1, 0, 32, "zxy"),
    (1, 0, 0, 32, "yxz"),
    (1, 1, 0, 16, "zyx"),
    (1, 1, 16, 16, "zxy"),
)
SIZES = {"x": NX, "y": NY, "z": NZ}


def coordinates():
    z = lax.axis_index("dp")
    ctx = lax.axis_index("ctx")
    core = lax.rem(ctx, 2)
    y = lax.rem(ctx // 2, NY)
    x = ctx // (2 * NY)
    return x, y, z, core


def place(x, y, z, core):
    return (z, (x * NY + y) * 2 + core)


def neighbour(x, y, z, core, axis, step):
    size = SIZES[axis]
    if axis == "x":
        x = lax.rem(x + step + size, size)
    elif axis == "y":
        y = lax.rem(y + step + size, size)
    else:
        z = lax.rem(z + step + size, size)
    return place(x, y, z, core)


def entry_barrier(targets):
    barrier = pltpu.get_barrier_semaphore()
    for target in targets:
        pl.semaphore_signal(barrier, inc=1, device_id=target, device_id_type=MESH)
    pl.semaphore_wait(barrier, len(targets))


class Sends:
    def __init__(self, send_sem, recv_sem):
        self.send_sem, self.recv_sem, self.count = send_sem, recv_sem, 0

    def make(self, src, dst, device):
        index = self.count
        self.count += 1
        return pltpu.make_async_remote_copy(
            src_ref=src,
            dst_ref=dst,
            send_sem=self.send_sem.at[index],
            recv_sem=self.recv_sem.at[index],
            device_id=device,
            device_id_type=MESH,
        )


def gather_steps(part, wbuf, coords, sends):
    half, block, row, rows, order = part
    own = dict(zip("xyz", coords[:3]))
    core = coords[3]
    done = []
    steps = []
    for axis in order:
        size = SIZES[axis]

        def view(offset, lo=0, count=rows, axis=axis, size=size, done=tuple(done)):
            index = [half]
            for name in "zxy":
                if name == axis:
                    index.append(lax.rem(own[name] + offset + size, size))
                elif name in done:
                    index.append(pl.ds(0, SIZES[name]))
                else:
                    index.append(own[name])
            index.append(pl.ds(row + lo, count))
            index.append(pl.ds(block * 128, 128))
            return wbuf.at[tuple(index)]

        right = neighbour(*own.values(), core, axis, 1)
        left = neighbour(*own.values(), core, axis, -1)
        for step in range(1, size // 2):
            a, b = view(1 - step), view(step - 1)
            steps.append([sends.make(a, a, right), sends.make(b, b, left)])
        last = size // 2
        if rows == 32:
            a, b = view(1 - last, 0, 16), view(last - 1, 16, 16)
            steps.append([sends.make(a, a, right), sends.make(b, b, left)])
        elif row == 0:
            a = view(1 - last)
            steps.append([sends.make(a, a, right)])
        else:
            b = view(last - 1)
            steps.append([sends.make(b, b, left)])
        done.append(axis)
    return steps


def project_kernel(
    q_ref, g_ref, x_ref, w_ref,
    qh_ref, gh_ref, kv_ref, wout_ref,
    wbuf, xbuf, kvown, send_sem, recv_sem, local_sem,
):
    coords = coordinates()
    x, y, z, core = coords
    other = 1 - core
    partner = place(x, y, z, other)
    sends = Sends(send_sem, recv_sem)
    entry_barrier(
        [partner] + [neighbour(*coords, axis, step) for axis in "xyz" for step in (1, -1)]
    )
    mine = pl.ds(pl.multiple_of(core * TOKENS, TOKENS), TOKENS)

    swaps = []
    for half in range(2):
        rows = pl.ds(pl.multiple_of(core * 16, 16), 16)
        target = wbuf.at[half, z, x, y, rows]
        source = w_ref.at[:, pl.ds(pl.multiple_of(half * 512 + other * 256, 256), 256)]
        copy = sends.make(source, target, partner)
        copy.start()
        swaps.append(copy)
        target[...] = w_ref[:, pl.ds(pl.multiple_of(half * 512 + core * 256, 256), 256)]
    for copy in swaps:
        copy.wait()

    parts = [gather_steps(part, wbuf, coords, sends) for part in PARTS]

    theirs = pl.ds(pl.multiple_of(other * HALF, HALF), HALF)
    ours = pl.ds(pl.multiple_of(core * HALF, HALF), HALF)
    background = [
        sends.make(x_ref, xbuf.at[mine], partner),
        sends.make(q_ref.at[:, theirs], qh_ref.at[mine], partner),
        sends.make(g_ref.at[:, theirs], gh_ref.at[mine], partner),
    ]
    locals_ = [
        pltpu.make_async_copy(x_ref, xbuf.at[mine], local_sem.at[0]),
        pltpu.make_async_copy(q_ref.at[:, ours], qh_ref.at[mine], local_sem.at[1]),
        pltpu.make_async_copy(g_ref.at[:, ours], gh_ref.at[mine], local_sem.at[2]),
    ]
    count = max(len(steps) for steps in parts)
    for step in range(count):
        for steps in parts:
            if step:
                for copy in steps[step - 1]:
                    copy.wait_recv()
            for copy in steps[step]:
                copy.start()
        if step == 0:
            for copy in background + locals_:
                copy.start()
    for steps in parts:
        for copy in steps[count - 1]:
            copy.wait_recv()
    background[0].wait_recv()
    locals_[0].wait()

    for half in range(2):
        def body(k, total, half=half):
            rows = pl.ds(pl.multiple_of(k * 512, 512), 512)
            return total + jnp.dot(
                xbuf[:, rows],
                wbuf[half, k].reshape(512, 256),
                preferred_element_type=F32,
            )
        total = lax.fori_loop(0, NZ, body, jnp.zeros((PAIR, 256), F32))
        for b in range(2):
            kvown[2 * half + b] = total[:, b * 128 : (b + 1) * 128].astype(BF16)

    right = neighbour(*coords, "y", 1)
    left = neighbour(*coords, "y", -1)
    down = neighbour(*coords, "x", 1)
    hop, r1a, r1b, l1a, l1b, r2, l2 = ([] for _ in range(7))
    for p in range(4):
        own, old = kvown.at[p], kv_ref.at[0, p]
        hop.append(sends.make(own, kv_ref.at[0, p], down))
        r1 = sends.make(own, kv_ref.at[3, p], right)
        r1a.append(r1)
        sends.count -= 1
        r1b.append(sends.make(old, kv_ref.at[3, p], right))
        l1a.append(sends.make(own, kv_ref.at[1, p], left))
        sends.count -= 1
        l1b.append(sends.make(old, kv_ref.at[1, p], left))
        r2.append(sends.make(kv_ref.at[3, p], kv_ref.at[2, p], right))
        l2.append(sends.make(kv_ref.at[1, p], kv_ref.at[2, p], left))
    keep = pltpu.make_async_copy(kvown, kv_ref.at[4], local_sem.at[3])
    keep.start()
    for p in range(4):
        hop[p].start()

        @pl.when(y < NY - 1)
        def _(p=p):
            r1a[p].start()

        @pl.when(y == 0)
        def _(p=p):
            l1a[p].start()

    wsends = []
    for half in range(2):
        cols = pl.ds(pl.multiple_of(half * 512 + core * 256, 256), 256)
        wsends.append(sends.make(wbuf.at[half], wout_ref.at[:, :, :, :, cols], partner))
        locals_.append(
            pltpu.make_async_copy(wbuf.at[half], wout_ref.at[:, :, :, :, cols], local_sem.at[4 + half])
        )
        wsends[-1].start()
        locals_[-1].start()

    for p in range(4):
        hop[p].wait_recv()

        @pl.when(y == NY - 1)
        def _(p=p):
            r1b[p].start()

        @pl.when(y > 0)
        def _(p=p):
            l1b[p].start()

    inner = (y == 1) | (y == 2)
    for p in range(4):
        r1a[p].wait_recv()
        l1a[p].wait_recv()

        @pl.when(inner)
        def _(p=p):
            r2[p].start()
            l2[p].start()

    for p in range(4):

        @pl.when(y >= NY // 2)
        def _(p=p):
            r2[p].wait_recv()

        @pl.when(y < NY // 2)
        def _(p=p):
            l2[p].wait_recv()

    for steps in parts:
        for copies in steps:
            for copy in copies:
                copy.wait_send()
    for p in range(4):
        hop[p].wait_send()
        r1a[p].wait_send()
        l1a[p].wait_send()

        @pl.when(inner)
        def _(p=p):
            r2[p].wait_send()
            l2[p].wait_send()

    for copy in background[1:]:
        copy.wait_recv()
    for copy in background:
        copy.wait_send()
    for copy in wsends:
        copy.wait()
    for copy in locals_[1:]:
        copy.wait()
    keep.wait()


def attend_kernel(
    lengths_ref, q_ref, g_ref, k_ref, v_ref,
    att_ref, dq_ref, dk_ref, dv_ref,
    bias, kt, vt,
):
    step = pl.program_id(0)
    head = lax.rem(step, GROUP)
    chip = lax.axis_index("ctx") // 2
    row = lax.broadcasted_iota(jnp.int32, (PAIR, PAIR), 0)
    col = lax.broadcasted_iota(jnp.int32, (PAIR, PAIR), 1)
    upper = row <= col

    @pl.when(step == 0)
    def _():
        position = chip * PAIR + lax.broadcasted_iota(jnp.int32, (1, PAIR), 1)
        end = jnp.int32(0)
        start = jnp.zeros((1, PAIR), jnp.int32)
        for n in range(lengths_ref.shape[1]):
            end = end + lengths_ref[0, n]
            start = jnp.where(position >= end, end, start)
        for s in range(4):
            base = chip * PAIR + row
            if s < 3:
                key = base - (3 - s) * PAIR
            else:
                key = jnp.where(upper, base, base - 4 * PAIR)
            bias[s] = jnp.where(key >= start, 0.0, -1e30)

    @pl.when(head == 0)
    def _():
        for s in range(5):
            kt[s] = k_ref[s, 0].T
            vt[s] = v_ref[s, 0].T

    q, g = q_ref[...], g_ref[...]
    nt = (((1,), (1,)), ((), ()))
    score = [
        lax.dot_general(k_ref[s, 0], q, nt, preferred_element_type=F32) for s in range(5)
    ]
    score = [*score[1:4], jnp.where(upper, score[4], score[0])]
    score = [t * (SCALE * LOG2E) + bias[s] for s, t in enumerate(score)]
    top = functools.reduce(jnp.maximum, [jnp.max(t, axis=0, keepdims=True) for t in score])
    weight = [jnp.exp2(t - top) for t in score]
    total = sum(jnp.sum(t, axis=0, keepdims=True) for t in weight)
    inverse = 1.0 / total

    def split(values):
        low = [t.astype(BF16) for t in values]
        zero = jnp.zeros_like(values[3])
        first = jnp.where(upper, zero, values[3]).astype(BF16)
        last = jnp.where(upper, values[3], zero).astype(BF16)
        return [first, *low[:3], last]

    mixed = sum(
        jnp.dot(vt[s], t, preferred_element_type=F32) for s, t in enumerate(split(weight))
    )
    out = (mixed * inverse).astype(BF16).astype(F32)
    att_ref[...] = out.T.astype(BF16)
    product = jnp.sum(g.astype(F32).T * out, axis=0, keepdims=True)
    pressure = [
        lax.dot_general(v_ref[s, 0], g, nt, preferred_element_type=F32) for s in range(5)
    ]
    pressure = [*pressure[1:4], jnp.where(upper, pressure[4], pressure[0])]
    prob = [t * inverse for t in weight]
    slope = split([t * (r - product) for t, r in zip(prob, pressure)])
    prob = split(prob)
    dq = sum(jnp.dot(kt[s], t, preferred_element_type=F32) for s, t in enumerate(slope))
    dq_ref[...] = (dq * SCALE).T.astype(BF16)
    for s in range(5):
        dk = jnp.dot(slope[s], q, preferred_element_type=F32) * SCALE
        dv = jnp.dot(prob[s], g, preferred_element_type=F32)

        @pl.when(head == 0)
        def _(s=s, dk=dk, dv=dv):
            dk_ref[s, 0] = dk
            dv_ref[s, 0] = dv

        @pl.when(head > 0)
        def _(s=s, dk=dk, dv=dv):
            dk_ref[s, 0] += dk
            dv_ref[s, 0] += dv


def reduce_kernel(
    dk_ref, dv_ref, att_ref, dq_ref, w_ref,
    out_ref, dqout_ref, ig_ref,
    part, wbuf, stage, land, flat, result, send_sem, recv_sem, local_sem,
):
    coords = coordinates()
    x, y, z, core = coords
    other = 1 - core
    partner = place(x, y, z, other)
    right = neighbour(*coords, "y", 1)
    left = neighbour(*coords, "y", -1)
    up = neighbour(*coords, "x", -1)
    down = neighbour(*coords, "x", 1)
    sends = Sends(send_sem, recv_sem)
    loads = [
        pltpu.make_async_copy(ref.at[s], part.at[s, pl.ds(2 * n, 2)], local_sem.at[2 * i + n])
        for i, s in enumerate((2, 3, 1, 0, 4))
        for n, ref in enumerate((dk_ref, dv_ref))
    ]
    for copy in loads:
        copy.start()
    entry_barrier([partner, right, left, up, down])
    weight = pltpu.make_async_copy(w_ref, wbuf, local_sem.at[10])
    weight.start()

    ours = pl.ds(pl.multiple_of(core * HALF, HALF), HALF)
    mine = pl.ds(pl.multiple_of(core * TOKENS, TOKENS), TOKENS)
    theirs = pl.ds(pl.multiple_of(other * TOKENS, TOKENS), TOKENS)

    inner = (y == 1) | (y == 2)
    high = y >= NY // 2
    low = y < NY // 2
    a_left = [sends.make(stage.at[0, p], land.at[0, p], left) for p in range(4)]
    a_right = [sends.make(stage.at[0, p], land.at[1, p], right) for p in range(4)]
    b_left = [sends.make(stage.at[1, p], land.at[2, p], left) for p in range(4)]
    b_right = [sends.make(stage.at[2, p], land.at[3, p], right) for p in range(4)]
    c_up = [sends.make(stage.at[3, p], land.at[4, p], up) for p in range(4)]

    for copy in loads[0:2]:
        copy.wait()
    for p in range(4):
        stage[0, p] = part[2, p].astype(BF16)

        @pl.when(high)
        def _(p=p):
            a_left[p].start()

        @pl.when(low)
        def _(p=p):
            a_right[p].start()

    outs = [
        sends.make(att_ref.at[theirs], out_ref.at[:, ours], partner),
        sends.make(dq_ref.at[theirs], dqout_ref.at[:, ours], partner),
    ]
    keeps = [
        pltpu.make_async_copy(att_ref.at[mine], out_ref.at[:, ours], local_sem.at[11]),
        pltpu.make_async_copy(dq_ref.at[mine], dqout_ref.at[:, ours], local_sem.at[12]),
    ]
    for copy in outs + keeps:
        copy.start()

    for copy in loads[2:6]:
        copy.wait()
    for p in range(4):
        @pl.when(inner)
        def _(p=p):
            a_left[p].wait_recv()
            a_right[p].wait_recv()
            stage[1, p] = (part[3, p] + land[0, p].astype(F32)).astype(BF16)
            stage[2, p] = (part[1, p] + land[1, p].astype(F32)).astype(BF16)

        @pl.when(jnp.logical_not(inner))
        def _(p=p):
            stage[1, p] = part[3, p].astype(BF16)
            stage[2, p] = part[1, p].astype(BF16)

        b_left[p].start()
        b_right[p].start()

    for copy in loads[6:10]:
        copy.wait()
    for p in range(4):
        b_left[p].wait_recv()
        b_right[p].wait_recv()
        from_right = land[2, p].astype(F32)
        from_left = land[3, p].astype(F32)
        before = part[0, p]
        before = before + jnp.where(y == NY - 1, from_right, 0.0)
        before = before + jnp.where(y > 0, from_left, 0.0)
        stage[3, p] = before.astype(BF16)
        c_up[p].start()
        own = part[4, p]
        own = own + jnp.where(y < NY - 1, from_right, 0.0)
        own = own + jnp.where(y == 0, from_left, 0.0)
        part[4, p] = own

    d = []
    for p in range(4):
        c_up[p].wait_recv()
        own = (part[4, p] + land[4, p].astype(F32)).astype(BF16)
        column = (p // 2) * 512 + core * 256 + (p % 2) * 128
        cols = pl.ds(pl.multiple_of(column, 128), 128)
        stage[4, p] = own
        flat[:, cols] = stage[4, p, mine]
        copy = sends.make(stage.at[4, p, theirs], flat.at[:, cols], partner)
        copy.start()
        d.append(copy)

    weight.wait()
    for copy in d:
        copy.wait_recv()

    def tile(n, carry):
        rows = pl.ds(pl.multiple_of(n * 512, 512), 512)
        result[:, rows] = lax.dot_general(
            flat[...], wbuf[rows], (((1,), (1,)), ((), ())), preferred_element_type=F32
        ).astype(BF16)
        return carry

    lax.fori_loop(0, MODEL // 512, tile, 0)
    final = pltpu.make_async_copy(result, ig_ref, local_sem.at[13])
    final.start()
    for copy in d:
        copy.wait_send()
    for p in range(4):

        @pl.when(high)
        def _(p=p):
            a_left[p].wait_send()

        @pl.when(low)
        def _(p=p):
            a_right[p].wait_send()

        b_left[p].wait_send()
        b_right[p].wait_send()
        c_up[p].wait_send()
    for copy in outs:
        copy.wait()
    for copy in keeps:
        copy.wait()
    final.wait()


def shards(queries, layer_input, key_value_weight, output_gradient, document_lengths):
    anywhere = pl.BlockSpec(memory_space=pl.ANY)
    whole = pl.BlockSpec(memory_space=pltpu.VMEM)
    shape = jax.ShapeDtypeStruct
    sems = pltpu.SemaphoreType.DMA
    qh, gh, kv, weight = pl.pallas_call(
        project_kernel,
        out_shape=(
            shape((PAIR, HALF), BF16),
            shape((PAIR, HALF), BF16),
            shape((5, 4, PAIR, HEAD_SIZE), BF16),
            shape((NZ, NX, NY, 32, 1024), BF16),
        ),
        in_specs=[anywhere, anywhere, anywhere, whole],
        out_specs=[anywhere] * 4,
        scratch_shapes=[
            pltpu.VMEM((2, NZ, NX, NY, 32, 256), BF16),
            pltpu.VMEM((PAIR, MODEL), BF16),
            pltpu.VMEM((4, PAIR, HEAD_SIZE), BF16),
            sems((128,)),
            sems((128,)),
            sems((8,)),
        ],
        compiler_params=pltpu.CompilerParams(
            collective_id=0, has_side_effects=True, vmem_limit_bytes=32 << 20
        ),
        name="project",
    )(queries[0], output_gradient[0], layer_input[0], key_value_weight)

    head_columns = pl.BlockSpec((PAIR, HEAD_SIZE), lambda n: (0, n))
    partial = pl.BlockSpec((5, 1, PAIR, HEAD_SIZE), lambda n: (0, n // GROUP, 0, 0))
    attended, dq, dk, dv = pl.pallas_call(
        attend_kernel,
        grid=(2 * GROUP,),
        out_shape=(
            shape((PAIR, HALF), BF16),
            shape((PAIR, HALF), BF16),
            shape((5, 2, PAIR, HEAD_SIZE), F32),
            shape((5, 2, PAIR, HEAD_SIZE), F32),
        ),
        in_specs=[
            pl.BlockSpec(memory_space=pltpu.SMEM),
            head_columns,
            head_columns,
            partial,
            pl.BlockSpec((5, 1, PAIR, HEAD_SIZE), lambda n: (0, 2 + n // GROUP, 0, 0)),
        ],
        out_specs=[head_columns, head_columns, partial, partial],
        scratch_shapes=[
            pltpu.VMEM((4, PAIR, PAIR), F32),
            pltpu.VMEM((5, HEAD_SIZE, PAIR), BF16),
            pltpu.VMEM((5, HEAD_SIZE, PAIR), BF16),
        ],
        compiler_params=pltpu.CompilerParams(vmem_limit_bytes=48 << 20),
        name="attend",
    )(document_lengths, qh, gh, kv, kv)

    out, dqout, ig = pl.pallas_call(
        reduce_kernel,
        out_shape=(
            shape((TOKENS, MODEL), BF16),
            shape((TOKENS, MODEL), BF16),
            shape((TOKENS, MODEL), BF16),
        ),
        in_specs=[anywhere] * 5,
        out_specs=[anywhere] * 3,
        scratch_shapes=[
            pltpu.VMEM((5, 4, PAIR, HEAD_SIZE), F32),
            pltpu.VMEM((MODEL, 1024), BF16),
            pltpu.VMEM((5, 4, PAIR, HEAD_SIZE), BF16),
            pltpu.VMEM((5, 4, PAIR, HEAD_SIZE), BF16),
            pltpu.VMEM((TOKENS, 1024), BF16),
            pltpu.VMEM((TOKENS, MODEL), BF16),
            sems((32,)),
            sems((32,)),
            sems((16,)),
        ],
        compiler_params=pltpu.CompilerParams(
            collective_id=1, has_side_effects=True, vmem_limit_bytes=40 << 20
        ),
        name="reduce",
    )(dk, dv, attended, dq, weight.reshape(MODEL, 1024))
    return (out[None], dqout[None], ig[None])


def solution(mesh):
    return jax.shard_map(
        shards,
        mesh=mesh,
        in_specs=(
            P("dp", "ctx", None),
            P("dp", "ctx", None),
            P(("dp", "ctx"), None),
            P("dp", "ctx", None),
            P("dp", None),
        ),
        out_specs=(P("dp", "ctx", None), P("dp", "ctx", None), P("dp", "ctx", None)),
        check_vma=False,
    )
```

```python
import functools
import math

import jax
import jax.numpy as jnp
from jax import lax
from jax.experimental import pallas as pl
from jax.experimental.pallas import tpu as pltpu
from jax.sharding import PartitionSpec as P

QUERY_HEADS = 32
KEY_VALUE_HEADS = 4
HEAD_SIZE = 128
GROUP = QUERY_HEADS // KEY_VALUE_HEADS
NX, NY, NZ = 4, 4, 8
TOKENS = 128
PAIR = 2 * TOKENS
MODEL = 4096
HALF = MODEL // 2
SCALE = 1.0 / math.sqrt(HEAD_SIZE)
LOG2E = math.log2(math.e)
TOGETHER = 2
MESH = pl.DeviceIdType.MESH
F32 = jnp.float32
BF16 = jnp.bfloat16

SIZES = {"x": NX, "y": NY, "z": NZ}


def coordinates():
    z = lax.axis_index("dp")
    ctx = lax.axis_index("ctx")
    core = lax.rem(ctx, 2)
    y = lax.rem(ctx // 2, NY)
    x = ctx // (2 * NY)
    return x, y, z, core


def place(x, y, z, core):
    return (z, (x * NY + y) * 2 + core)


def neighbour(x, y, z, core, axis, step):
    size = SIZES[axis]
    if axis == "x":
        x = lax.rem(x + step + size, size)
    elif axis == "y":
        y = lax.rem(y + step + size, size)
    else:
        z = lax.rem(z + step + size, size)
    return place(x, y, z, core)


def entry_barrier(targets):
    barrier = pltpu.get_barrier_semaphore()
    for target in targets:
        pl.semaphore_signal(barrier, inc=1, device_id=target, device_id_type=MESH)
    pl.semaphore_wait(barrier, len(targets))


class Sends:
    def __init__(self, send_sem, recv_sem):
        self.send_sem, self.recv_sem, self.count = send_sem, recv_sem, 0

    def make(self, src, dst, device):
        index = self.count
        self.count += 1
        return pltpu.make_async_remote_copy(
            src_ref=src,
            dst_ref=dst,
            send_sem=self.send_sem.at[index],
            recv_sem=self.recv_sem.at[index],
            device_id=device,
            device_id_type=MESH,
        )


def fan(axis):
    size = SIZES[axis]
    return sorted(range(1 - size // 2, size // 2 + 1), key=abs)[1:]


def layer_kernel(
    lengths_ref, q_ref, g_ref, x_ref, w_ref,
    att_ref, dq_ref, ig_ref,
    wbuf, wother, xbuf, qsend, gsend, qh, gh, kv, bias, kt, vt, dkt, dvt, prob_ref, slope_ref,
    part, stage, land, flat, acc, atts, dqs, attr, dqr, igs, igr, send_sem, recv_sem, local_sem,
):
    coords = coordinates()
    x, y, z, core = coords
    other = 1 - core
    chip = x * NY + y
    partner = place(x, y, z, other)
    sends = Sends(send_sem, recv_sem)
    started = []

    def go(copy):
        copy.start()
        started.append(copy)
        return copy

    locals_count = [0]

    def local(src, dst):
        copy = pltpu.make_async_copy(src, dst, local_sem.at[locals_count[0]])
        locals_count[0] += 1
        copy.start()
        return copy

    def at(axis, step):
        return neighbour(*coords, axis, step)

    def index(axis, step):
        return lax.rem({"x": x, "y": y, "z": z}[axis] + step + SIZES[axis], SIZES[axis])

    mine = pl.ds(pl.multiple_of(core * TOKENS, TOKENS), TOKENS)
    yours = pl.ds(pl.multiple_of(other * TOKENS, TOKENS), TOKENS)
    ours = pl.ds(pl.multiple_of(core * HALF, HALF), HALF)
    theirs = pl.ds(pl.multiple_of(other * HALF, HALF), HALF)

    loads = [
        local(x_ref, xbuf.at[mine]),
        local(q_ref.at[:, theirs], qsend),
        local(g_ref.at[:, theirs], gsend),
        local(q_ref.at[:, ours], qh.at[mine]),
        local(g_ref.at[:, ours], gh.at[mine]),
    ]
    entry_barrier(
        [partner] + [at(axis, step) for axis in "xyz" for step in fan(axis)]
    )

    rows = pl.ds(pl.multiple_of(core * 16, 16), 16)
    swaps = []
    for a in range(2):
        for b in range(2):
            target = wbuf.at[a, z, x, y, rows, pl.ds(b * 128, 128)]
            away = pl.multiple_of(b * 512 + other * 256 + a * 128, 128)
            here = pl.multiple_of(b * 512 + core * 256 + a * 128, 128)
            swaps.append(go(sends.make(w_ref.at[:, pl.ds(away, 128)], target, partner)))
            target[...] = w_ref[:, pl.ds(here, 128)]
    for copy in swaps:
        copy.wait_recv()

    zfan = [
        go(sends.make(wbuf.at[0, z, x, y], wbuf.at[0, z, x, y], at("z", step)))
        for step in fan("z")
    ]
    yfan = [
        go(sends.make(wbuf.at[1, z, x, y], wbuf.at[1, z, x, y], at("y", step)))
        for step in fan("y")
    ]
    for copy in loads[:3]:
        copy.wait()
    swapx = go(sends.make(xbuf.at[mine], xbuf.at[mine], partner))
    swapq = go(sends.make(qsend, qh.at[mine], partner))
    swapg = go(sends.make(gsend, gh.at[mine], partner))
    for copy in yfan:
        copy.wait_recv()
    xfan = [
        go(sends.make(wbuf.at[1, z, x], wbuf.at[1, z, x], at("x", step)))
        for step in fan("x")
    ]
    for copy in zfan:
        copy.wait_recv()

    def keys_of(i, j):
        return wbuf.at[0, :, i, j, :, pl.ds(0, 128)]

    def values_of(i, j):
        return wbuf.at[0, :, i, j, :, pl.ds(128, 128)]

    first, second = [], []
    for step in fan("y"):
        first.append(
            (
                go(sends.make(keys_of(x, y), keys_of(x, y), at("y", step))),
                go(sends.make(values_of(x, y), values_of(x, y), at("x", step))),
            )
        )

    def onward(step):
        j, i = index("y", -step), index("x", -step)
        for to in fan("x"):
            second.append(go(sends.make(keys_of(x, j), keys_of(x, j), at("x", to))))
            second.append(go(sends.make(values_of(i, y), values_of(i, y), at("y", to))))

    onward(0)
    for step, (one, two) in zip(fan("y"), first):
        one.wait_recv()
        two.wait_recv()
        onward(step)
    for copy in xfan:
        copy.wait_recv()

    ring = []

    def round_z(step):
        copies = []
        for piece in range(2):
            half = pl.ds(piece * 2, 2)
            back = wbuf.at[1, index("z", 1 - step), half]
            ahead = wbuf.at[1, index("z", step - 1), half]
            if ring:
                for copy in ring[-1][2 * piece : 2 * piece + 2]:
                    copy.wait_recv()
            if step < NZ // 2 or piece == 0:
                copies.append(go(sends.make(back, back, at("z", 1))))
            if step < NZ // 2 or piece == 1:
                copies.append(go(sends.make(ahead, ahead, at("z", -1))))
        ring.append(copies)

    round_z(1)
    for copy in second:
        copy.wait_recv()
    swapx.wait_recv()

    def project(a):
        def body(k, total):
            columns = pl.ds(pl.multiple_of(k * 512, 512), 512)
            return total + jnp.dot(
                xbuf[:, columns], wbuf[a, k].reshape(512, 256), preferred_element_type=F32
            )
        total = lax.fori_loop(0, NZ, body, jnp.zeros((PAIR, 256), F32))
        for b in range(2):
            kv[2 * a + b, 4] = total[:, b * 128 : (b + 1) * 128].astype(BF16)

    def pass_on(a):
        hops, near, far = [], [], []
        for p in (2 * a, 2 * a + 1):
            hops.append(go(sends.make(kv.at[p, 4], kv.at[p, 0], at("x", 1))))
            for k in (1, 2, 3):
                near.append(sends.make(kv.at[p, 4], kv.at[p, 4 - k], at("y", k)))
                sends.count -= 1
                far.append(sends.make(kv.at[p, 0], kv.at[p, 4 - k], at("y", k)))

                @pl.when(y + k < NY)
                def _(copy=near[-1]):
                    copy.start()

                started.append(near[-1])
        half = pl.ds(pl.multiple_of(other * 4, 4), 4)
        whole = go(sends.make(wbuf.at[a, half], wother.at[a], partner))
        return hops, near, far, whole

    def pass_far(passed):
        hops, near, far, whole = passed
        for n, hop in enumerate(hops):
            hop.wait_recv()
            for k in (1, 2, 3):

                @pl.when(y + k >= NY)
                def _(copy=far[3 * n + k - 1]):
                    copy.start()

    def passed_all(passed):
        for copy in passed[1]:
            copy.wait_recv()

    row = lax.broadcasted_iota(jnp.int32, (PAIR, PAIR), 0)
    col = lax.broadcasted_iota(jnp.int32, (PAIR, PAIR), 1)
    nt = (((1,), (1,)), ((), ()))

    project(0)
    passed = pass_on(0)

    position = chip * PAIR + lax.broadcasted_iota(jnp.int32, (1, PAIR), 1)
    end = jnp.int32(0)
    start = jnp.zeros((1, PAIR), jnp.int32)
    for n in range(lengths_ref.shape[1]):
        end = end + lengths_ref[0, n]
        start = jnp.where(position >= end, end, start)
    for s in range(4):
        base = chip * PAIR + row
        if s < 3:
            key = base - (3 - s) * PAIR
        else:
            key = jnp.where(row <= col, base, base - 4 * PAIR)
        bias[s] = jnp.where(key >= start, 0.0, -1e30)

    round_z(2)
    pass_far(passed)
    for copy in loads[3:]:
        copy.wait()
    swapq.wait_recv()
    swapg.wait_recv()
    passed_all(passed)

    def prepare(a):
        kt[...] = kv[2 * a].reshape(5 * PAIR, HEAD_SIZE).T
        vt[...] = kv[2 * a + 1].reshape(5 * PAIR, HEAD_SIZE).T
        dkt[...] = jnp.zeros_like(dkt)
        dvt[...] = jnp.zeros_like(dvt)

    upper = jnp.concatenate([row <= col] * TOGETHER, axis=1)

    def attend(a, step):
        columns = [
            pl.ds(
                pl.multiple_of((a * GROUP + step * TOGETHER + n) * HEAD_SIZE, HEAD_SIZE),
                HEAD_SIZE,
            )
            for n in range(TOGETHER)
        ]
        q = jnp.concatenate([qh[:, c] for c in columns], axis=0)
        g = jnp.concatenate([gh[:, c] for c in columns], axis=0)
        gt = g.T
        keys = kv[2 * a].reshape(5 * PAIR, HEAD_SIZE)
        values = kv[2 * a + 1].reshape(5 * PAIR, HEAD_SIZE)

        def blocks(u, v):
            t = lax.dot_general(u, v, nt, preferred_element_type=F32)
            t = [t[s * PAIR : (s + 1) * PAIR] for s in range(5)]
            return [*t[1:4], jnp.where(upper, t[4], t[0])]

        score = [
            t * (SCALE * LOG2E) + jnp.concatenate([bias[s]] * TOGETHER, axis=1)
            for s, t in enumerate(blocks(keys, q))
        ]
        top = functools.reduce(
            jnp.maximum, [jnp.max(t, axis=0, keepdims=True) for t in score]
        )
        weight = [jnp.exp2(t - top) for t in score]
        total = sum(jnp.sum(t, axis=0, keepdims=True) for t in weight)
        inverse = 1.0 / total

        def split(ref, parts):
            for s in range(3):
                ref[(s + 1) * PAIR : (s + 2) * PAIR] = parts[s].astype(BF16)
            ref[0:PAIR] = jnp.where(upper, 0.0, parts[3]).astype(BF16)
            ref[4 * PAIR : 5 * PAIR] = jnp.where(upper, parts[3], 0.0).astype(BF16)

        split(prob_ref, weight)
        mixed = jnp.dot(vt[...], prob_ref[...], preferred_element_type=F32)
        out = (mixed * inverse).astype(BF16).astype(F32)
        for n, c in enumerate(columns):
            atts[:, c] = out[:, n * PAIR : (n + 1) * PAIR].T.astype(BF16)
        product = jnp.sum(gt.astype(F32) * out, axis=0, keepdims=True)
        prob = [t * inverse for t in weight]
        split(slope_ref, [t * (r - product) for t, r in zip(prob, blocks(values, g))])
        split(prob_ref, prob)
        dq = jnp.dot(kt[...], slope_ref[...], preferred_element_type=F32) * SCALE
        for n, c in enumerate(columns):
            dqs[:, c] = dq[:, n * PAIR : (n + 1) * PAIR].T.astype(BF16)
        dkt[...] += lax.dot_general(q.T, slope_ref[...], nt, preferred_element_type=F32)
        dvt[...] += lax.dot_general(gt, prob_ref[...], nt, preferred_element_type=F32)

    def attend_two(a, first):
        lax.fori_loop(first, first + 2, lambda n, c: (attend(a, n), c)[1], 0)

    outs, keeps = [], []

    def finish(a):
        part[2 * a] = (dkt[...] * SCALE).T.reshape(5, PAIR, HEAD_SIZE)
        part[2 * a + 1] = dvt[...].T.reshape(5, PAIR, HEAD_SIZE)
        returns = []
        for p in (2 * a, 2 * a + 1):
            for k in (1, 2, 3):
                stage[p, k] = part[p, 4 - k].astype(BF16)
                returns.append(go(sends.make(stage.at[p, k], land.at[p, k], at("y", -k))))
        cols = pl.ds(a * HALF // 2, HALF // 2)
        for src, dst, ref in ((atts, attr, att_ref), (dqs, dqr, dq_ref)):
            outs.append(go(sends.make(src.at[yours, cols], dst.at[:, cols], partner)))
            place_cols = pl.ds(pl.multiple_of(core * HALF + a * HALF // 2, HALF // 2), HALF // 2)
            keeps.append(local(src.at[mine, cols], ref.at[:, place_cols]))
        return returns

    def collect(a, returns):
        ups = []
        for b in range(2):
            p = 2 * a + b
            before, own = part[p, 0], part[p, 4]
            for k in (1, 2, 3):
                returns[3 * b + k - 1].wait_recv()
                value = land[p, k].astype(F32)
                before = before + jnp.where(y + k >= NY, value, 0.0)
                own = own + jnp.where(y + k < NY, value, 0.0)
            stage[p, 0] = before.astype(BF16)
            part[p, 4] = own
            ups.append(go(sends.make(stage.at[p, 0], land.at[p, 0], at("x", -1))))
        return ups

    def settle(a, ups):
        crosses = []
        for b in range(2):
            p = 2 * a + b
            ups[b].wait_recv()
            cols = pl.ds(b * 128, 128)
            block = flat.at[core * 2 + a, :, cols]
            block[...] = (part[p, 4] + land[p, 0].astype(F32)).astype(BF16)
            crosses.append(go(sends.make(block, block, partner)))
        return crosses

    def multiply(a, n):
        total = lax.dot_general(
            flat[core * 2 + a], wbuf[a, core * 4 + n].reshape(512, 256), nt,
            preferred_element_type=F32,
        )
        return total + lax.dot_general(
            flat[other * 2 + a], wother[a, n].reshape(512, 256), nt,
            preferred_element_type=F32,
        )

    prepare(0)
    attend_two(0, 0)
    round_z(3)
    attend(0, 2)
    round_z(4)
    attend(0, 3)
    returns0 = finish(0)
    for copy in ring[-1]:
        copy.wait_recv()
    project(1)
    passed1 = pass_on(1)
    ups0 = collect(0, returns0)
    pass_far(passed1)
    crosses0 = settle(0, ups0)
    passed_all(passed1)
    prepare(1)
    attend_two(1, 0)
    for copy in crosses0:
        copy.wait_recv()
    passed[3].wait_recv()
    attend_two(1, 2)
    returns1 = finish(1)
    passed1[3].wait_recv()
    for n in range(4):
        acc[:, n * 512 : (n + 1) * 512] = multiply(0, n)
    ups1 = collect(1, returns1)
    for copy in settle(1, ups1):
        copy.wait_recv()
    sends_ig = []
    for n in range(4):
        cols = slice(n * 512, (n + 1) * 512)
        igs[:, cols] = (acc[:, cols] + multiply(1, n)).astype(BF16)
        sends_ig.append(
            go(sends.make(igs.at[yours, pl.ds(n * 512, 512)], igr.at[:, pl.ds(n * 512, 512)], partner))
        )
    keeps.append(local(igs.at[mine], ig_ref.at[:, ours]))
    for copy in outs:
        copy.wait_recv()
    keeps.append(local(attr, att_ref.at[:, theirs]))
    keeps.append(local(dqr, dq_ref.at[:, theirs]))
    for copy in sends_ig:
        copy.wait_recv()
    keeps.append(local(igr, ig_ref.at[:, theirs]))
    for copy in started:
        copy.wait_send()
    for copy in keeps:
        copy.wait()


def shards(queries, layer_input, key_value_weight, output_gradient, document_lengths):
    anywhere = pl.BlockSpec(memory_space=pl.ANY)
    shape = jax.ShapeDtypeStruct((TOKENS, MODEL), BF16)
    sems = pltpu.SemaphoreType.DMA
    window = 5 * PAIR
    wide = TOGETHER * PAIR
    att, dq, ig = pl.pallas_call(
        layer_kernel,
        out_shape=(shape,) * 3,
        in_specs=[
            pl.BlockSpec(memory_space=pltpu.SMEM),
            anywhere,
            anywhere,
            anywhere,
            pl.BlockSpec(memory_space=pltpu.VMEM),
        ],
        out_specs=[anywhere] * 3,
        scratch_shapes=[
            pltpu.VMEM((2, NZ, NX, NY, 32, 256), BF16),
            pltpu.VMEM((2, NZ // 2, NX, NY, 32, 256), BF16),
            pltpu.VMEM((PAIR, MODEL), BF16),
            pltpu.VMEM((TOKENS, HALF), BF16),
            pltpu.VMEM((TOKENS, HALF), BF16),
            pltpu.VMEM((PAIR, HALF), BF16),
            pltpu.VMEM((PAIR, HALF), BF16),
            pltpu.VMEM((4, 5, PAIR, HEAD_SIZE), BF16),
            pltpu.VMEM((4, PAIR, PAIR), F32),
            pltpu.VMEM((HEAD_SIZE, window), BF16),
            pltpu.VMEM((HEAD_SIZE, window), BF16),
            pltpu.VMEM((HEAD_SIZE, window), F32),
            pltpu.VMEM((HEAD_SIZE, window), F32),
            pltpu.VMEM((window, wide), BF16),
            pltpu.VMEM((window, wide), BF16),
            pltpu.VMEM((4, 5, PAIR, HEAD_SIZE), F32),
            pltpu.VMEM((4, 4, PAIR, HEAD_SIZE), BF16),
            pltpu.VMEM((4, 4, PAIR, HEAD_SIZE), BF16),
            pltpu.VMEM((4, PAIR, 256), BF16),
            pltpu.VMEM((PAIR, HALF), F32),
            pltpu.VMEM((PAIR, HALF), BF16),
            pltpu.VMEM((PAIR, HALF), BF16),
            pltpu.VMEM((TOKENS, HALF), BF16),
            pltpu.VMEM((TOKENS, HALF), BF16),
            pltpu.VMEM((PAIR, HALF), BF16),
            pltpu.VMEM((TOKENS, HALF), BF16),
            sems((160,)),
            sems((160,)),
            sems((24,)),
        ],
        compiler_params=pltpu.CompilerParams(
            collective_id=0, has_side_effects=True, vmem_limit_bytes=61 << 20
        ),
        name="layer",
    )(document_lengths, queries[0], output_gradient[0], layer_input[0], key_value_weight)
    return (att[None], dq[None], ig[None])


def solution(mesh):
    return jax.shard_map(
        shards,
        mesh=mesh,
        in_specs=(
            P("dp", "ctx", None),
            P("dp", "ctx", None),
            P(("dp", "ctx"), None),
            P("dp", "ctx", None),
            P("dp", None),
        ),
        out_specs=(P("dp", "ctx", None), P("dp", "ctx", None), P("dp", "ctx", None)),
        check_vma=False,
    )
```

```python
import functools
import math

import jax
import jax.numpy as jnp
from jax import lax
from jax.experimental import pallas as pl
from jax.experimental.pallas import tpu as pltpu
from jax.sharding import PartitionSpec as P

QUERY_HEADS = 32
KEY_VALUE_HEADS = 4
HEAD_SIZE = 128
GROUP = QUERY_HEADS // KEY_VALUE_HEADS
NX, NY, NZ = 4, 4, 8
TOKENS = 128
PAIR = 2 * TOKENS
MODEL = 4096
HALF = MODEL // 2
SCALE = 1.0 / math.sqrt(HEAD_SIZE)
LOG2E = math.log2(math.e)
TOGETHER = 2
MESH = pl.DeviceIdType.MESH
F32 = jnp.float32
BF16 = jnp.bfloat16

SIZES = {"x": NX, "y": NY, "z": NZ}


def coordinates():
    z = lax.axis_index("dp")
    ctx = lax.axis_index("ctx")
    core = lax.rem(ctx, 2)
    y = lax.rem(ctx // 2, NY)
    x = ctx // (2 * NY)
    return x, y, z, core


def place(x, y, z, core):
    return (z, (x * NY + y) * 2 + core)


def neighbour(x, y, z, core, axis, step):
    size = SIZES[axis]
    if axis == "x":
        x = lax.rem(x + step + size, size)
    elif axis == "y":
        y = lax.rem(y + step + size, size)
    else:
        z = lax.rem(z + step + size, size)
    return place(x, y, z, core)


def entry_barrier(targets):
    barrier = pltpu.get_barrier_semaphore()
    for target in targets:
        pl.semaphore_signal(barrier, inc=1, device_id=target, device_id_type=MESH)
    pl.semaphore_wait(barrier, len(targets))


class Sends:
    def __init__(self, send_sem, recv_sem):
        self.send_sem, self.recv_sem, self.count = send_sem, recv_sem, 0

    def make(self, src, dst, device):
        index = self.count
        self.count += 1
        return pltpu.make_async_remote_copy(
            src_ref=src,
            dst_ref=dst,
            send_sem=self.send_sem.at[index],
            recv_sem=self.recv_sem.at[index],
            device_id=device,
            device_id_type=MESH,
        )


def fan(axis):
    size = SIZES[axis]
    return sorted(range(1 - size // 2, size // 2 + 1), key=abs)[1:]


def layer_kernel(
    lengths_ref, q_ref, g_ref, x_ref, w_ref,
    att_ref, dq_ref, ig_ref,
    wbuf, wother, xbuf, qsend, gsend, qh, gh, kv, bias, kt, vt, dkt, dvt, prob_ref, slope_ref,
    part, stage, land, flat, acc, atts, dqs, attr, dqr, igs, igr, send_sem, recv_sem, local_sem,
):
    coords = coordinates()
    x, y, z, core = coords
    other = 1 - core
    chip = x * NY + y
    partner = place(x, y, z, other)
    sends = Sends(send_sem, recv_sem)
    started = []

    def go(copy):
        copy.start()
        started.append(copy)
        return copy

    locals_count = [0]

    def local(src, dst):
        copy = pltpu.make_async_copy(src, dst, local_sem.at[locals_count[0]])
        locals_count[0] += 1
        copy.start()
        return copy

    def at(axis, step):
        return neighbour(*coords, axis, step)

    def index(axis, step):
        return lax.rem({"x": x, "y": y, "z": z}[axis] + step + SIZES[axis], SIZES[axis])

    mine = pl.ds(pl.multiple_of(core * TOKENS, TOKENS), TOKENS)
    yours = pl.ds(pl.multiple_of(other * TOKENS, TOKENS), TOKENS)
    ours = pl.ds(pl.multiple_of(core * HALF, HALF), HALF)
    theirs = pl.ds(pl.multiple_of(other * HALF, HALF), HALF)

    loads = [
        local(x_ref, xbuf.at[mine]),
        local(q_ref.at[:, theirs], qsend),
        local(g_ref.at[:, theirs], gsend),
        local(q_ref.at[:, ours], qh.at[mine]),
        local(g_ref.at[:, ours], gh.at[mine]),
    ]
    entry_barrier(
        [partner] + [at(axis, step) for axis in "xyz" for step in fan(axis)]
    )

    rows = pl.ds(pl.multiple_of(core * 16, 16), 16)
    swaps = []
    for a in range(2):
        for b in range(2):
            target = wbuf.at[a, z, x, y, rows, pl.ds(b * 128, 128)]
            away = pl.multiple_of(b * 512 + other * 256 + a * 128, 128)
            here = pl.multiple_of(b * 512 + core * 256 + a * 128, 128)
            swaps.append(go(sends.make(w_ref.at[:, pl.ds(away, 128)], target, partner)))
            target[...] = w_ref[:, pl.ds(here, 128)]
    for copy in swaps:
        copy.wait_recv()

    zfan = [
        go(sends.make(wbuf.at[0, z, x, y], wbuf.at[0, z, x, y], at("z", step)))
        for step in fan("z")
    ]
    yfan = [
        go(sends.make(wbuf.at[1, z, x, y], wbuf.at[1, z, x, y], at("y", step)))
        for step in fan("y")
    ]
    for copy in loads[:3]:
        copy.wait()
    swapx = go(sends.make(xbuf.at[mine], xbuf.at[mine], partner))
    swapq = go(sends.make(qsend, qh.at[mine], partner))
    swapg = go(sends.make(gsend, gh.at[mine], partner))
    for copy in yfan:
        copy.wait_recv()
    xfan = [
        go(sends.make(wbuf.at[1, z, x], wbuf.at[1, z, x], at("x", step)))
        for step in fan("x")
    ]
    for copy in zfan:
        copy.wait_recv()

    def keys_of(i, j):
        return wbuf.at[0, :, i, j, :, pl.ds(0, 128)]

    def values_of(i, j):
        return wbuf.at[0, :, i, j, :, pl.ds(128, 128)]

    first, second = [], []
    for step in fan("y"):
        first.append(
            (
                go(sends.make(keys_of(x, y), keys_of(x, y), at("y", step))),
                go(sends.make(values_of(x, y), values_of(x, y), at("x", step))),
            )
        )

    def onward(step):
        j, i = index("y", -step), index("x", -step)
        for to in fan("x"):
            second.append(go(sends.make(keys_of(x, j), keys_of(x, j), at("x", to))))
            second.append(go(sends.make(values_of(i, y), values_of(i, y), at("y", to))))

    onward(0)
    for step, (one, two) in zip(fan("y"), first):
        one.wait_recv()
        two.wait_recv()
        onward(step)
    for copy in xfan:
        copy.wait_recv()

    ring = []

    def round_z(step):
        copies = []
        for piece in range(2):
            half = pl.ds(piece * 2, 2)
            back = wbuf.at[1, index("z", 1 - step), half]
            ahead = wbuf.at[1, index("z", step - 1), half]
            if ring:
                for copy in ring[-1][2 * piece : 2 * piece + 2]:
                    copy.wait_recv()
            if step < NZ // 2 or piece == 0:
                copies.append(go(sends.make(back, back, at("z", 1))))
            if step < NZ // 2 or piece == 1:
                copies.append(go(sends.make(ahead, ahead, at("z", -1))))
        ring.append(copies)

    round_z(1)
    for n, copy in enumerate(second):
        if n in (6, 18):
            round_z(2 if n == 6 else 3)
        copy.wait_recv()
    swapx.wait_recv()

    def project(a):
        def body(k, total):
            columns = pl.ds(pl.multiple_of(k * 512, 512), 512)
            return total + jnp.dot(
                xbuf[:, columns], wbuf[a, k].reshape(512, 256), preferred_element_type=F32
            )
        total = lax.fori_loop(0, NZ, body, jnp.zeros((PAIR, 256), F32))
        for b in range(2):
            kv[2 * a + b, 4] = total[:, b * 128 : (b + 1) * 128].astype(BF16)

    def pass_on(a):
        hops, near, far = [], [], []
        for p in (2 * a, 2 * a + 1):
            hops.append(go(sends.make(kv.at[p, 4], kv.at[p, 0], at("x", 1))))
            for k in (1, 2, 3):
                near.append(sends.make(kv.at[p, 4], kv.at[p, 4 - k], at("y", k)))
                sends.count -= 1
                far.append(sends.make(kv.at[p, 0], kv.at[p, 4 - k], at("y", k)))

                @pl.when(y + k < NY)
                def _(copy=near[-1]):
                    copy.start()

                started.append(near[-1])
        half = pl.ds(pl.multiple_of(other * 4, 4), 4)
        whole = go(sends.make(wbuf.at[a, half], wother.at[a], partner))
        return hops, near, far, whole

    def pass_far(passed):
        hops, near, far, whole = passed
        for n, hop in enumerate(hops):
            hop.wait_recv()
            for k in (1, 2, 3):

                @pl.when(y + k >= NY)
                def _(copy=far[3 * n + k - 1]):
                    copy.start()

    def passed_all(passed):
        for copy in passed[1]:
            copy.wait_recv()

    row = lax.broadcasted_iota(jnp.int32, (PAIR, PAIR), 0)
    col = lax.broadcasted_iota(jnp.int32, (PAIR, PAIR), 1)
    nt = (((1,), (1,)), ((), ()))

    project(0)
    passed = pass_on(0)

    position = chip * PAIR + lax.broadcasted_iota(jnp.int32, (1, PAIR), 1)
    end = jnp.int32(0)
    start = jnp.zeros((1, PAIR), jnp.int32)
    for n in range(lengths_ref.shape[1]):
        end = end + lengths_ref[0, n]
        start = jnp.where(position >= end, end, start)
    for s in range(4):
        base = chip * PAIR + row
        if s < 3:
            key = base - (3 - s) * PAIR
        else:
            key = jnp.where(row <= col, base, base - 4 * PAIR)
        bias[s] = jnp.where(key >= start, 0.0, -1e30)

    pass_far(passed)
    round_z(4)
    for copy in loads[3:]:
        copy.wait()
    swapq.wait_recv()
    swapg.wait_recv()
    passed_all(passed)

    def prepare(a):
        kt[...] = kv[2 * a].reshape(5 * PAIR, HEAD_SIZE).T
        vt[...] = kv[2 * a + 1].reshape(5 * PAIR, HEAD_SIZE).T
        dkt[...] = jnp.zeros_like(dkt)
        dvt[...] = jnp.zeros_like(dvt)

    upper = jnp.concatenate([row <= col] * TOGETHER, axis=1)

    def attend(a, step):
        columns = [
            pl.ds(
                pl.multiple_of((a * GROUP + step * TOGETHER + n) * HEAD_SIZE, HEAD_SIZE),
                HEAD_SIZE,
            )
            for n in range(TOGETHER)
        ]
        q = jnp.concatenate([qh[:, c] for c in columns], axis=0)
        g = jnp.concatenate([gh[:, c] for c in columns], axis=0)
        gt = g.T
        keys = kv[2 * a].reshape(5 * PAIR, HEAD_SIZE)
        values = kv[2 * a + 1].reshape(5 * PAIR, HEAD_SIZE)

        def blocks(u, v):
            t = lax.dot_general(u, v, nt, preferred_element_type=F32)
            t = [t[s * PAIR : (s + 1) * PAIR] for s in range(5)]
            return [*t[1:4], jnp.where(upper, t[4], t[0])]

        score = [
            t * (SCALE * LOG2E) + jnp.concatenate([bias[s]] * TOGETHER, axis=1)
            for s, t in enumerate(blocks(keys, q))
        ]
        top = functools.reduce(
            jnp.maximum, [jnp.max(t, axis=0, keepdims=True) for t in score]
        )
        weight = [jnp.exp2(t - top) for t in score]
        total = sum(jnp.sum(t, axis=0, keepdims=True) for t in weight)
        inverse = 1.0 / total

        def split(ref, parts):
            for s in range(3):
                ref[(s + 1) * PAIR : (s + 2) * PAIR] = parts[s].astype(BF16)
            ref[0:PAIR] = jnp.where(upper, 0.0, parts[3]).astype(BF16)
            ref[4 * PAIR : 5 * PAIR] = jnp.where(upper, parts[3], 0.0).astype(BF16)

        split(prob_ref, weight)
        mixed = jnp.dot(vt[...], prob_ref[...], preferred_element_type=F32)
        out = (mixed * inverse).astype(BF16).astype(F32)
        for n, c in enumerate(columns):
            atts[:, c] = out[:, n * PAIR : (n + 1) * PAIR].T.astype(BF16)
        product = jnp.sum(gt.astype(F32) * out, axis=0, keepdims=True)
        prob = [t * inverse for t in weight]
        split(slope_ref, [t * (r - product) for t, r in zip(prob, blocks(values, g))])
        split(prob_ref, prob)
        dq = jnp.dot(kt[...], slope_ref[...], preferred_element_type=F32) * SCALE
        for n, c in enumerate(columns):
            dqs[:, c] = dq[:, n * PAIR : (n + 1) * PAIR].T.astype(BF16)
        dkt[...] += lax.dot_general(q.T, slope_ref[...], nt, preferred_element_type=F32)
        dvt[...] += lax.dot_general(gt, prob_ref[...], nt, preferred_element_type=F32)

    def attend_two(a, first):
        lax.fori_loop(first, first + 2, lambda n, c: (attend(a, n), c)[1], 0)

    outs, keeps = [], []

    def finish(a):
        part[2 * a] = (dkt[...] * SCALE).T.reshape(5, PAIR, HEAD_SIZE)
        part[2 * a + 1] = dvt[...].T.reshape(5, PAIR, HEAD_SIZE)
        returns = []
        for p in (2 * a, 2 * a + 1):
            for k in (1, 2, 3):
                stage[p, k] = part[p, 4 - k].astype(BF16)
                returns.append(go(sends.make(stage.at[p, k], land.at[p, k], at("y", -k))))
        cols = pl.ds(a * HALF // 2, HALF // 2)
        for src, dst, ref in ((atts, attr, att_ref), (dqs, dqr, dq_ref)):
            outs.append(go(sends.make(src.at[yours, cols], dst.at[:, cols], partner)))
            place_cols = pl.ds(pl.multiple_of(core * HALF + a * HALF // 2, HALF // 2), HALF // 2)
            keeps.append(local(src.at[mine, cols], ref.at[:, place_cols]))
        return returns

    def collect(a, returns):
        ups = []
        for b in range(2):
            p = 2 * a + b
            before, own = part[p, 0], part[p, 4]
            for k in (1, 2, 3):
                returns[3 * b + k - 1].wait_recv()
                value = land[p, k].astype(F32)
                before = before + jnp.where(y + k >= NY, value, 0.0)
                own = own + jnp.where(y + k < NY, value, 0.0)
            stage[p, 0] = before.astype(BF16)
            part[p, 4] = own
            ups.append(go(sends.make(stage.at[p, 0], land.at[p, 0], at("x", -1))))
        return ups

    def settle(a, ups):
        crosses = []
        for b in range(2):
            p = 2 * a + b
            ups[b].wait_recv()
            cols = pl.ds(b * 128, 128)
            block = flat.at[core * 2 + a, :, cols]
            block[...] = (part[p, 4] + land[p, 0].astype(F32)).astype(BF16)
            crosses.append(go(sends.make(block, block, partner)))
        return crosses

    def multiply(a, n):
        total = lax.dot_general(
            flat[core * 2 + a], wbuf[a, core * 4 + n].reshape(512, 256), nt,
            preferred_element_type=F32,
        )
        return total + lax.dot_general(
            flat[other * 2 + a], wother[a, n].reshape(512, 256), nt,
            preferred_element_type=F32,
        )

    prepare(0)
    attend(0, 0)
    for copy in ring[-1]:
        copy.wait_recv()
    project(1)
    passed1 = pass_on(1)
    attend(0, 1)
    attend(0, 2)
    pass_far(passed1)
    attend(0, 3)
    returns0 = finish(0)
    passed_all(passed1)
    prepare(1)
    attend_two(1, 0)
    ups0 = collect(0, returns0)
    attend(1, 2)
    crosses0 = settle(0, ups0)
    attend(1, 3)
    for copy in crosses0:
        copy.wait_recv()
    passed[3].wait_recv()
    returns1 = finish(1)
    passed1[3].wait_recv()
    for n in range(4):
        acc[:, n * 512 : (n + 1) * 512] = multiply(0, n)
    ups1 = collect(1, returns1)
    for copy in settle(1, ups1):
        copy.wait_recv()
    sends_ig = []
    for n in range(4):
        cols = slice(n * 512, (n + 1) * 512)
        igs[:, cols] = (acc[:, cols] + multiply(1, n)).astype(BF16)
        sends_ig.append(
            go(sends.make(igs.at[yours, pl.ds(n * 512, 512)], igr.at[:, pl.ds(n * 512, 512)], partner))
        )
    keeps.append(local(igs.at[mine], ig_ref.at[:, ours]))
    for copy in outs:
        copy.wait_recv()
    keeps.append(local(attr, att_ref.at[:, theirs]))
    keeps.append(local(dqr, dq_ref.at[:, theirs]))
    for copy in sends_ig:
        copy.wait_recv()
    keeps.append(local(igr, ig_ref.at[:, theirs]))
    for copy in started:
        copy.wait_send()
    for copy in keeps:
        copy.wait()


def shards(queries, layer_input, key_value_weight, output_gradient, document_lengths):
    anywhere = pl.BlockSpec(memory_space=pl.ANY)
    shape = jax.ShapeDtypeStruct((TOKENS, MODEL), BF16)
    sems = pltpu.SemaphoreType.DMA
    window = 5 * PAIR
    wide = TOGETHER * PAIR
    att, dq, ig = pl.pallas_call(
        layer_kernel,
        out_shape=(shape,) * 3,
        in_specs=[
            pl.BlockSpec(memory_space=pltpu.SMEM),
            anywhere,
            anywhere,
            anywhere,
            pl.BlockSpec(memory_space=pltpu.VMEM),
        ],
        out_specs=[anywhere] * 3,
        scratch_shapes=[
            pltpu.VMEM((2, NZ, NX, NY, 32, 256), BF16),
            pltpu.VMEM((2, NZ // 2, NX, NY, 32, 256), BF16),
            pltpu.VMEM((PAIR, MODEL), BF16),
            pltpu.VMEM((TOKENS, HALF), BF16),
            pltpu.VMEM((TOKENS, HALF), BF16),
            pltpu.VMEM((PAIR, HALF), BF16),
            pltpu.VMEM((PAIR, HALF), BF16),
            pltpu.VMEM((4, 5, PAIR, HEAD_SIZE), BF16),
            pltpu.VMEM((4, PAIR, PAIR), F32),
            pltpu.VMEM((HEAD_SIZE, window), BF16),
            pltpu.VMEM((HEAD_SIZE, window), BF16),
            pltpu.VMEM((HEAD_SIZE, window), F32),
            pltpu.VMEM((HEAD_SIZE, window), F32),
            pltpu.VMEM((window, wide), BF16),
            pltpu.VMEM((window, wide), BF16),
            pltpu.VMEM((4, 5, PAIR, HEAD_SIZE), F32),
            pltpu.VMEM((4, 4, PAIR, HEAD_SIZE), BF16),
            pltpu.VMEM((4, 4, PAIR, HEAD_SIZE), BF16),
            pltpu.VMEM((4, PAIR, 256), BF16),
            pltpu.VMEM((PAIR, HALF), F32),
            pltpu.VMEM((PAIR, HALF), BF16),
            pltpu.VMEM((PAIR, HALF), BF16),
            pltpu.VMEM((TOKENS, HALF), BF16),
            pltpu.VMEM((TOKENS, HALF), BF16),
            pltpu.VMEM((PAIR, HALF), BF16),
            pltpu.VMEM((TOKENS, HALF), BF16),
            sems((160,)),
            sems((160,)),
            sems((24,)),
        ],
        compiler_params=pltpu.CompilerParams(
            collective_id=0, has_side_effects=True, vmem_limit_bytes=61 << 20
        ),
        name="layer",
    )(document_lengths, queries[0], output_gradient[0], layer_input[0], key_value_weight)
    return (att[None], dq[None], ig[None])


def solution(mesh):
    return jax.shard_map(
        shards,
        mesh=mesh,
        in_specs=(
            P("dp", "ctx", None),
            P("dp", "ctx", None),
            P(("dp", "ctx"), None),
            P("dp", "ctx", None),
            P("dp", None),
        ),
        out_specs=(P("dp", "ctx", None), P("dp", "ctx", None), P("dp", "ctx", None)),
        check_vma=False,
    )
```

```python
import functools
import math

import jax
import jax.numpy as jnp
from jax import lax
from jax.experimental import pallas as pl
from jax.experimental.pallas import tpu as pltpu
from jax.sharding import PartitionSpec as P

QUERY_HEADS = 32
KEY_VALUE_HEADS = 4
HEAD_SIZE = 128
GROUP = QUERY_HEADS // KEY_VALUE_HEADS
NX, NY, NZ = 4, 4, 8
TOKENS = 128
PAIR = 2 * TOKENS
MODEL = 4096
HALF = MODEL // 2
SCALE = 1.0 / math.sqrt(HEAD_SIZE)
LOG2E = math.log2(math.e)
TOGETHER = 2
MESH = pl.DeviceIdType.MESH
F32 = jnp.float32
BF16 = jnp.bfloat16

SIZES = {"x": NX, "y": NY, "z": NZ}


def coordinates():
    z = lax.axis_index("dp")
    ctx = lax.axis_index("ctx")
    core = lax.rem(ctx, 2)
    y = lax.rem(ctx // 2, NY)
    x = ctx // (2 * NY)
    return x, y, z, core


def place(x, y, z, core):
    return (z, (x * NY + y) * 2 + core)


def neighbour(x, y, z, core, axis, step):
    size = SIZES[axis]
    if axis == "x":
        x = lax.rem(x + step + size, size)
    elif axis == "y":
        y = lax.rem(y + step + size, size)
    else:
        z = lax.rem(z + step + size, size)
    return place(x, y, z, core)


def entry_barrier(targets):
    barrier = pltpu.get_barrier_semaphore()
    for target in targets:
        pl.semaphore_signal(barrier, inc=1, device_id=target, device_id_type=MESH)
    pl.semaphore_wait(barrier, len(targets))


class Sends:
    def __init__(self, send_sem, recv_sem):
        self.send_sem, self.recv_sem, self.count = send_sem, recv_sem, 0

    def make(self, src, dst, device):
        index = self.count
        self.count += 1
        return pltpu.make_async_remote_copy(
            src_ref=src,
            dst_ref=dst,
            send_sem=self.send_sem.at[index],
            recv_sem=self.recv_sem.at[index],
            device_id=device,
            device_id_type=MESH,
        )


def fan(axis):
    size = SIZES[axis]
    return sorted(range(1 - size // 2, size // 2 + 1), key=abs)[1:]


def layer_kernel(
    lengths_ref, q_ref, g_ref, x_ref, w_ref,
    att_ref, dq_ref, ig_ref,
    wbuf, wother, xbuf, qsend, gsend, qh, gh, kv, bias, kt, vt, dkt, dvt, prob_ref, slope_ref,
    part, stage, land, flat, acc, atts, dqs, igs, send_sem, recv_sem, local_sem,
):
    coords = coordinates()
    x, y, z, core = coords
    other = 1 - core
    chip = x * NY + y
    partner = place(x, y, z, other)
    sends = Sends(send_sem, recv_sem)
    started = []

    def go(copy):
        copy.start()
        started.append(copy)
        return copy

    locals_count = [0]

    def local(src, dst):
        copy = pltpu.make_async_copy(src, dst, local_sem.at[locals_count[0]])
        locals_count[0] += 1
        copy.start()
        return copy

    def at(axis, step):
        return neighbour(*coords, axis, step)

    def index(axis, step):
        return lax.rem({"x": x, "y": y, "z": z}[axis] + step + SIZES[axis], SIZES[axis])

    mine = pl.ds(pl.multiple_of(core * TOKENS, TOKENS), TOKENS)
    yours = pl.ds(pl.multiple_of(other * TOKENS, TOKENS), TOKENS)
    ours = pl.ds(pl.multiple_of(core * HALF, HALF), HALF)
    theirs = pl.ds(pl.multiple_of(other * HALF, HALF), HALF)

    loads = [
        local(x_ref, xbuf.at[mine]),
        local(q_ref.at[:, theirs], qsend),
        local(g_ref.at[:, theirs], gsend),
        local(q_ref.at[:, ours], qh.at[mine]),
        local(g_ref.at[:, ours], gh.at[mine]),
    ]
    entry_barrier(
        [partner] + [at(axis, step) for axis in "xyz" for step in fan(axis)]
    )

    rows = pl.ds(pl.multiple_of(core * 16, 16), 16)
    swaps = []
    for a in range(2):
        for b in range(2):
            target = wbuf.at[a, z, x, y, rows, pl.ds(b * 128, 128)]
            away = pl.multiple_of(b * 512 + other * 256 + a * 128, 128)
            here = pl.multiple_of(b * 512 + core * 256 + a * 128, 128)
            swaps.append(go(sends.make(w_ref.at[:, pl.ds(away, 128)], target, partner)))
            target[...] = w_ref[:, pl.ds(here, 128)]
    for copy in swaps:
        copy.wait_recv()

    zfan = [
        go(sends.make(wbuf.at[0, z, x, y], wbuf.at[0, z, x, y], at("z", step)))
        for step in fan("z")
    ]
    yfan = [
        go(sends.make(wbuf.at[1, z, x, y], wbuf.at[1, z, x, y], at("y", step)))
        for step in fan("y")
    ]
    for copy in loads[:3]:
        copy.wait()
    swapx = go(sends.make(xbuf.at[mine], xbuf.at[mine], partner))
    swapq = go(sends.make(qsend, qh.at[mine], partner))
    swapg = go(sends.make(gsend, gh.at[mine], partner))
    for copy in yfan:
        copy.wait_recv()
    xfan = [
        go(sends.make(wbuf.at[1, z, x], wbuf.at[1, z, x], at("x", step)))
        for step in fan("x")
    ]
    for copy in zfan:
        copy.wait_recv()

    def keys_of(i, j):
        return wbuf.at[0, :, i, j, :, pl.ds(0, 128)]

    def values_of(i, j):
        return wbuf.at[0, :, i, j, :, pl.ds(128, 128)]

    first, second = [], []
    for step in fan("y"):
        first.append(
            (
                go(sends.make(keys_of(x, y), keys_of(x, y), at("y", step))),
                go(sends.make(values_of(x, y), values_of(x, y), at("x", step))),
            )
        )

    def onward(step):
        j, i = index("y", -step), index("x", -step)
        for to in fan("x"):
            second.append(go(sends.make(keys_of(x, j), keys_of(x, j), at("x", to))))
            second.append(go(sends.make(values_of(i, y), values_of(i, y), at("y", to))))

    onward(0)
    for step, (one, two) in zip(fan("y"), first):
        one.wait_recv()
        two.wait_recv()
        onward(step)
    for copy in xfan:
        copy.wait_recv()

    ring = []

    def round_z(step):
        copies = []
        for piece in range(2):
            half = pl.ds(piece * 2, 2)
            back = wbuf.at[1, index("z", 1 - step), half]
            ahead = wbuf.at[1, index("z", step - 1), half]
            if ring:
                for copy in ring[-1][2 * piece : 2 * piece + 2]:
                    copy.wait_recv()
            if step < NZ // 2 or piece == 0:
                copies.append(go(sends.make(back, back, at("z", 1))))
            if step < NZ // 2 or piece == 1:
                copies.append(go(sends.make(ahead, ahead, at("z", -1))))
        ring.append(copies)

    round_z(1)
    for n, copy in enumerate(second):
        if n in (6, 18):
            round_z(2 if n == 6 else 3)
        copy.wait_recv()
    swapx.wait_recv()

    def project(a):
        total = jnp.dot(
            xbuf[...], wbuf[a].reshape(MODEL, 256), preferred_element_type=F32
        )
        for b in range(2):
            kv[2 * a + b, 4] = total[:, b * 128 : (b + 1) * 128].astype(BF16)

    def pass_on(a):
        hops, near, far = [], [], []
        for p in (2 * a, 2 * a + 1):
            hops.append(go(sends.make(kv.at[p, 4], kv.at[p, 0], at("x", 1))))
            for k in (1, 2, 3):
                near.append(sends.make(kv.at[p, 4], kv.at[p, 4 - k], at("y", k)))
                sends.count -= 1
                far.append(sends.make(kv.at[p, 0], kv.at[p, 4 - k], at("y", k)))

                @pl.when(y + k < NY)
                def _(copy=near[-1]):
                    copy.start()

                started.append(near[-1])
        half = pl.ds(pl.multiple_of(other * 4, 4), 4)
        whole = go(sends.make(wbuf.at[a, half], wother.at[a], partner))
        return hops, near, far, whole

    def pass_far(passed):
        hops, near, far, whole = passed
        for n, hop in enumerate(hops):
            hop.wait_recv()
            for k in (1, 2, 3):

                @pl.when(y + k >= NY)
                def _(copy=far[3 * n + k - 1]):
                    copy.start()

    def passed_some(passed, b):
        for copy in passed[1][3 * b : 3 * b + 3]:
            copy.wait_recv()

    row = lax.broadcasted_iota(jnp.int32, (PAIR, PAIR), 0)
    col = lax.broadcasted_iota(jnp.int32, (PAIR, PAIR), 1)
    nt = (((1,), (1,)), ((), ()))

    project(0)
    passed = pass_on(0)

    position = chip * PAIR + lax.broadcasted_iota(jnp.int32, (1, PAIR), 1)
    end = jnp.int32(0)
    start = jnp.zeros((1, PAIR), jnp.int32)
    for n in range(lengths_ref.shape[1]):
        end = end + lengths_ref[0, n]
        start = jnp.where(position >= end, end, start)
    for s in range(4):
        base = chip * PAIR + row
        if s < 3:
            key = base - (3 - s) * PAIR
        else:
            key = jnp.where(row <= col, base, base - 4 * PAIR)
        bias[s] = jnp.where(key >= start, 0.0, -1e30)

    pass_far(passed)
    round_z(4)
    for copy in loads[3:]:
        copy.wait()
    swapq.wait_recv()
    swapg.wait_recv()
    passed_some(passed, 0)

    def prepare(a):
        kt[...] = kv[2 * a].reshape(5 * PAIR, HEAD_SIZE).T
        dkt[...] = jnp.zeros_like(dkt)
        dvt[...] = jnp.zeros_like(dvt)

    upper = jnp.concatenate([row <= col] * TOGETHER, axis=1)

    def attend(a, step, passed=None, leave=None):
        columns = [
            pl.ds(
                pl.multiple_of((a * GROUP + step * TOGETHER + n) * HEAD_SIZE, HEAD_SIZE),
                HEAD_SIZE,
            )
            for n in range(TOGETHER)
        ]
        q = jnp.concatenate([qh[:, c] for c in columns], axis=0)
        g = jnp.concatenate([gh[:, c] for c in columns], axis=0)
        gt = g.T
        keys = kv[2 * a].reshape(5 * PAIR, HEAD_SIZE)

        def blocks(u, v):
            t = lax.dot_general(u, v, nt, preferred_element_type=F32)
            t = [t[s * PAIR : (s + 1) * PAIR] for s in range(5)]
            return [*t[1:4], jnp.where(upper, t[4], t[0])]

        score = [
            t * (SCALE * LOG2E) + jnp.concatenate([bias[s]] * TOGETHER, axis=1)
            for s, t in enumerate(blocks(keys, q))
        ]
        top = functools.reduce(
            jnp.maximum, [jnp.max(t, axis=0, keepdims=True) for t in score]
        )
        weight = [jnp.exp2(t - top) for t in score]
        total = sum(jnp.sum(t, axis=0, keepdims=True) for t in weight)
        inverse = 1.0 / total

        def split(ref, parts):
            for s in range(3):
                ref[(s + 1) * PAIR : (s + 2) * PAIR] = parts[s].astype(BF16)
            ref[0:PAIR] = jnp.where(upper, 0.0, parts[3]).astype(BF16)
            ref[4 * PAIR : 5 * PAIR] = jnp.where(upper, parts[3], 0.0).astype(BF16)

        split(prob_ref, weight)
        if passed is not None:
            passed_some(passed, 1)
            vt[...] = kv[2 * a + 1].reshape(5 * PAIR, HEAD_SIZE).T
        mixed = jnp.dot(vt[...], prob_ref[...], preferred_element_type=F32)
        out = (mixed * inverse).astype(BF16).astype(F32)
        for n, c in enumerate(columns):
            atts[:, c] = out[:, n * PAIR : (n + 1) * PAIR].T.astype(BF16)
        product = jnp.sum(gt.astype(F32) * out, axis=0, keepdims=True)
        prob = [t * inverse for t in weight]
        split(prob_ref, prob)
        dvt[...] += lax.dot_general(gt, prob_ref[...], nt, preferred_element_type=F32)
        if leave is not None:
            leave(a, 1)
        values = kv[2 * a + 1].reshape(5 * PAIR, HEAD_SIZE)
        split(slope_ref, [t * (r - product) for t, r in zip(prob, blocks(values, g))])
        dq = jnp.dot(kt[...], slope_ref[...], preferred_element_type=F32) * SCALE
        for n, c in enumerate(columns):
            dqs[:, c] = dq[:, n * PAIR : (n + 1) * PAIR].T.astype(BF16)
        dkt[...] += lax.dot_general(q.T, slope_ref[...], nt, preferred_element_type=F32)

    def attend_two(a, first):
        lax.fori_loop(first, first + 2, lambda n, c: (attend(a, n), c)[1], 0)

    outs, keeps = [], []
    returns = {}

    def leave(a, b):
        p = 2 * a + b
        part[p] = (dvt[...] if b else dkt[...] * SCALE).T.reshape(5, PAIR, HEAD_SIZE)
        for k in (1, 2, 3):
            stage[p, k] = part[p, 4 - k].astype(BF16)
            returns[p, k] = go(sends.make(stage.at[p, k], land.at[p, k], at("y", -k)))

    def finish(a):
        leave(a, 0)
        cols = pl.ds(a * HALF // 2, HALF // 2)
        for src, ref in ((atts, att_ref), (dqs, dq_ref)):
            place_cols = pl.ds(pl.multiple_of(core * HALF + a * HALF // 2, HALF // 2), HALF // 2)
            outs.append(go(sends.make(src.at[yours, cols], ref.at[:, place_cols], partner)))
            keeps.append(local(src.at[mine, cols], ref.at[:, place_cols]))

    def collect(a):
        ups = {}
        for b in (1, 0):
            p = 2 * a + b
            before, own = part[p, 0], part[p, 4]
            for k in (1, 2, 3):
                returns[p, k].wait_recv()
                value = land[p, k].astype(F32)
                before = before + jnp.where(y + k >= NY, value, 0.0)
                own = own + jnp.where(y + k < NY, value, 0.0)
            stage[p, 0] = before.astype(BF16)
            part[p, 4] = own
            ups[b] = go(sends.make(stage.at[p, 0], land.at[p, 0], at("x", -1)))
        return ups

    def settle(a, ups):
        crosses = []
        for b in (1, 0):
            p = 2 * a + b
            ups[b].wait_recv()
            cols = pl.ds(b * 128, 128)
            block = flat.at[core * 2 + a, :, cols]
            block[...] = (part[p, 4] + land[p, 0].astype(F32)).astype(BF16)
            crosses.append(go(sends.make(block, block, partner)))
        return crosses

    def multiply(a, n):
        total = lax.dot_general(
            flat[core * 2 + a], wbuf[a, core * 4 + n].reshape(512, 256), nt,
            preferred_element_type=F32,
        )
        return total + lax.dot_general(
            flat[other * 2 + a], wother[a, n].reshape(512, 256), nt,
            preferred_element_type=F32,
        )

    prepare(0)
    attend(0, 0, passed)
    for copy in ring[-1]:
        copy.wait_recv()
    project(1)
    passed1 = pass_on(1)
    attend(0, 1)
    attend(0, 2)
    pass_far(passed1)
    attend(0, 3, None, leave)
    finish(0)
    passed_some(passed1, 0)
    prepare(1)
    attend(1, 0, passed1)
    attend(1, 1)
    ups0 = collect(0)
    attend(1, 2)
    crosses0 = settle(0, ups0)
    attend(1, 3, None, leave)
    for copy in crosses0:
        copy.wait_recv()
    passed[3].wait_recv()
    finish(1)
    passed1[3].wait_recv()
    for n in range(4):
        acc[:, n * 512 : (n + 1) * 512] = multiply(0, n)
    ups1 = collect(1)
    for copy in settle(1, ups1):
        copy.wait_recv()
    for n in range(4):
        cols = pl.ds(n * 512, 512)
        placed = pl.ds(pl.multiple_of(core * HALF + n * 512, 512), 512)
        igs[:, cols] = (acc[:, cols] + multiply(1, n)).astype(BF16)
        outs.append(go(sends.make(igs.at[yours, cols], ig_ref.at[:, placed], partner)))
        keeps.append(local(igs.at[mine, cols], ig_ref.at[:, placed]))
    for copy in outs:
        copy.wait_recv()
    for copy in started:
        copy.wait_send()
    for copy in keeps:
        copy.wait()


def shards(queries, layer_input, key_value_weight, output_gradient, document_lengths):
    anywhere = pl.BlockSpec(memory_space=pl.ANY)
    shape = jax.ShapeDtypeStruct((TOKENS, MODEL), BF16)
    sems = pltpu.SemaphoreType.DMA
    window = 5 * PAIR
    wide = TOGETHER * PAIR
    att, dq, ig = pl.pallas_call(
        layer_kernel,
        out_shape=(shape,) * 3,
        in_specs=[
            pl.BlockSpec(memory_space=pltpu.SMEM),
            anywhere,
            anywhere,
            anywhere,
            pl.BlockSpec(memory_space=pltpu.VMEM),
        ],
        out_specs=[anywhere] * 3,
        scratch_shapes=[
            pltpu.VMEM((2, NZ, NX, NY, 32, 256), BF16),
            pltpu.VMEM((2, NZ // 2, NX, NY, 32, 256), BF16),
            pltpu.VMEM((PAIR, MODEL), BF16),
            pltpu.VMEM((TOKENS, HALF), BF16),
            pltpu.VMEM((TOKENS, HALF), BF16),
            pltpu.VMEM((PAIR, HALF), BF16),
            pltpu.VMEM((PAIR, HALF), BF16),
            pltpu.VMEM((4, 5, PAIR, HEAD_SIZE), BF16),
            pltpu.VMEM((4, PAIR, PAIR), F32),
            pltpu.VMEM((HEAD_SIZE, window), BF16),
            pltpu.VMEM((HEAD_SIZE, window), BF16),
            pltpu.VMEM((HEAD_SIZE, window), F32),
            pltpu.VMEM((HEAD_SIZE, window), F32),
            pltpu.VMEM((window, wide), BF16),
            pltpu.VMEM((window, wide), BF16),
            pltpu.VMEM((4, 5, PAIR, HEAD_SIZE), F32),
            pltpu.VMEM((4, 4, PAIR, HEAD_SIZE), BF16),
            pltpu.VMEM((4, 4, PAIR, HEAD_SIZE), BF16),
            pltpu.VMEM((4, PAIR, 256), BF16),
            pltpu.VMEM((PAIR, HALF), F32),
            pltpu.VMEM((PAIR, HALF), BF16),
            pltpu.VMEM((PAIR, HALF), BF16),
            pltpu.VMEM((PAIR, HALF), BF16),
            sems((160,)),
            sems((160,)),
            sems((24,)),
        ],
        compiler_params=pltpu.CompilerParams(
            collective_id=0, has_side_effects=True, vmem_limit_bytes=50 << 20
        ),
        name="layer",
    )(document_lengths, queries[0], output_gradient[0], layer_input[0], key_value_weight)
    return (att[None], dq[None], ig[None])


def solution(mesh):
    return jax.shard_map(
        shards,
        mesh=mesh,
        in_specs=(
            P("dp", "ctx", None),
            P("dp", "ctx", None),
            P(("dp", "ctx"), None),
            P("dp", "ctx", None),
            P("dp", None),
        ),
        out_specs=(P("dp", "ctx", None), P("dp", "ctx", None), P("dp", "ctx", None)),
        check_vma=False,
    )
```

```python
import functools
import math

import jax
import jax.numpy as jnp
from jax import lax
from jax.experimental import pallas as pl
from jax.experimental.pallas import tpu as pltpu
from jax.sharding import PartitionSpec as P

QUERY_HEADS = 32
KEY_VALUE_HEADS = 4
HEAD_SIZE = 128
GROUP = QUERY_HEADS // KEY_VALUE_HEADS
NX, NY, NZ = 4, 4, 8
TOKENS = 128
PAIR = 2 * TOKENS
MODEL = 4096
HALF = MODEL // 2
SCALE = 1.0 / math.sqrt(HEAD_SIZE)
LOG2E = math.log2(math.e)
TOGETHER = 2
MESH = pl.DeviceIdType.MESH
F32 = jnp.float32
BF16 = jnp.bfloat16

SIZES = {"x": NX, "y": NY, "z": NZ}


def coordinates():
    z = lax.axis_index("dp")
    ctx = lax.axis_index("ctx")
    core = lax.rem(ctx, 2)
    y = lax.rem(ctx // 2, NY)
    x = ctx // (2 * NY)
    return x, y, z, core


def place(x, y, z, core):
    return (z, (x * NY + y) * 2 + core)


def neighbour(x, y, z, core, axis, step):
    size = SIZES[axis]
    if axis == "x":
        x = lax.rem(x + step + size, size)
    elif axis == "y":
        y = lax.rem(y + step + size, size)
    else:
        z = lax.rem(z + step + size, size)
    return place(x, y, z, core)


def entry_barrier(targets):
    barrier = pltpu.get_barrier_semaphore()
    for target in targets:
        pl.semaphore_signal(barrier, inc=1, device_id=target, device_id_type=MESH)
    pl.semaphore_wait(barrier, len(targets))


class Sends:
    def __init__(self, send_sem, recv_sem):
        self.send_sem, self.recv_sem, self.count = send_sem, recv_sem, 0

    def make(self, src, dst, device):
        index = self.count
        self.count += 1
        return pltpu.make_async_remote_copy(
            src_ref=src,
            dst_ref=dst,
            send_sem=self.send_sem.at[index],
            recv_sem=self.recv_sem.at[index],
            device_id=device,
            device_id_type=MESH,
        )


def fan(axis):
    size = SIZES[axis]
    return sorted(range(1 - size // 2, size // 2 + 1), key=abs)[:0:-1]


def layer_kernel(
    lengths_ref, q_ref, g_ref, x_ref, w_ref,
    att_ref, dq_ref, ig_ref,
    wbuf, wother, xbuf, qsend, gsend, qh, gh, kv, bias, kt, vt, dkt, dvt, prob_ref, slope_ref,
    part, stage, land, flat, acc, atts, dqs, igs, send_sem, recv_sem, local_sem,
):
    coords = coordinates()
    x, y, z, core = coords
    other = 1 - core
    chip = x * NY + y
    partner = place(x, y, z, other)
    sends = Sends(send_sem, recv_sem)
    started = []

    def go(copy):
        copy.start()
        started.append(copy)
        return copy

    locals_count = [0]

    def local(src, dst):
        copy = pltpu.make_async_copy(src, dst, local_sem.at[locals_count[0]])
        locals_count[0] += 1
        copy.start()
        return copy

    def at(axis, step):
        return neighbour(*coords, axis, step)

    def index(axis, step):
        return lax.rem({"x": x, "y": y, "z": z}[axis] + step + SIZES[axis], SIZES[axis])

    mine = pl.ds(pl.multiple_of(core * TOKENS, TOKENS), TOKENS)
    yours = pl.ds(pl.multiple_of(other * TOKENS, TOKENS), TOKENS)
    ours = pl.ds(pl.multiple_of(core * HALF, HALF), HALF)
    theirs = pl.ds(pl.multiple_of(other * HALF, HALF), HALF)

    loads = [
        local(x_ref, xbuf.at[mine]),
        local(q_ref.at[:, theirs], qsend),
        local(g_ref.at[:, theirs], gsend),
        local(q_ref.at[:, ours], qh.at[mine]),
        local(g_ref.at[:, ours], gh.at[mine]),
    ]
    entry_barrier(
        [partner] + [at(axis, step) for axis in "xyz" for step in fan(axis)]
    )

    rows = pl.ds(pl.multiple_of(core * 16, 16), 16)
    swaps = []
    for a in range(2):
        for b in range(2):
            target = wbuf.at[a, z, x, y, rows, pl.ds(b * 128, 128)]
            away = pl.multiple_of(b * 512 + other * 256 + a * 128, 128)
            here = pl.multiple_of(b * 512 + core * 256 + a * 128, 128)
            swaps.append(go(sends.make(w_ref.at[:, pl.ds(away, 128)], target, partner)))
            target[...] = w_ref[:, pl.ds(here, 128)]
    for copy in swaps:
        copy.wait_recv()

    zfan = [
        go(sends.make(wbuf.at[0, z, x, y], wbuf.at[0, z, x, y], at("z", step)))
        for step in fan("z")
    ]
    yfan = [
        go(sends.make(wbuf.at[1, z, x, y], wbuf.at[1, z, x, y], at("y", step)))
        for step in fan("y")
    ]
    for copy in loads[:3]:
        copy.wait()
    swapx = go(sends.make(xbuf.at[mine], xbuf.at[mine], partner))
    swapq = go(sends.make(qsend, qh.at[mine], partner))
    swapg = go(sends.make(gsend, gh.at[mine], partner))
    for copy in yfan:
        copy.wait_recv()
    xfan = [
        go(sends.make(wbuf.at[1, z, x], wbuf.at[1, z, x], at("x", step)))
        for step in fan("x")
    ]
    for copy in zfan:
        copy.wait_recv()

    def keys_of(i, j):
        return wbuf.at[0, :, i, j, :, pl.ds(0, 128)]

    def values_of(i, j):
        return wbuf.at[0, :, i, j, :, pl.ds(128, 128)]

    first, second = [], []
    for step in fan("y"):
        first.append(
            (
                go(sends.make(keys_of(x, y), keys_of(x, y), at("y", step))),
                go(sends.make(values_of(x, y), values_of(x, y), at("x", step))),
            )
        )

    def onward(step):
        j, i = index("y", -step), index("x", -step)
        for to in fan("x"):
            second.append(go(sends.make(keys_of(x, j), keys_of(x, j), at("x", to))))
            second.append(go(sends.make(values_of(i, y), values_of(i, y), at("y", to))))

    onward(0)
    for step, (one, two) in zip(fan("y"), first):
        one.wait_recv()
        two.wait_recv()
        onward(step)
    for copy in xfan:
        copy.wait_recv()

    ring = []

    def round_z(step):
        copies = []
        for piece in range(2):
            half = pl.ds(piece * 2, 2)
            back = wbuf.at[1, index("z", 1 - step), half]
            ahead = wbuf.at[1, index("z", step - 1), half]
            if ring:
                for copy in ring[-1][2 * piece : 2 * piece + 2]:
                    copy.wait_recv()
            if step < NZ // 2 or piece == 0:
                copies.append(go(sends.make(back, back, at("z", 1))))
            if step < NZ // 2 or piece == 1:
                copies.append(go(sends.make(ahead, ahead, at("z", -1))))
        ring.append(copies)

    round_z(1)
    for n, copy in enumerate(second):
        if n in (6, 18):
            round_z(2 if n == 6 else 3)
        copy.wait_recv()
    swapx.wait_recv()

    def project(a):
        total = jnp.dot(
            xbuf[...], wbuf[a].reshape(MODEL, 256), preferred_element_type=F32
        )
        for b in range(2):
            kv[2 * a + b, 4] = total[:, b * 128 : (b + 1) * 128].astype(BF16)

    def pass_on(a):
        hops, near, far = [], [], []
        for p in (2 * a, 2 * a + 1):
            hops.append(go(sends.make(kv.at[p, 4], kv.at[p, 0], at("x", 1))))
            for k in (1, 2, 3):
                near.append(sends.make(kv.at[p, 4], kv.at[p, 4 - k], at("y", k)))
                sends.count -= 1
                far.append(sends.make(kv.at[p, 0], kv.at[p, 4 - k], at("y", k)))

                @pl.when(y + k < NY)
                def _(copy=near[-1]):
                    copy.start()

                started.append(near[-1])
        half = pl.ds(pl.multiple_of(other * 4, 4), 4)
        whole = go(sends.make(wbuf.at[a, half], wother.at[a], partner))
        return hops, near, far, whole

    def pass_far(passed):
        hops, near, far, whole = passed
        for n, hop in enumerate(hops):
            hop.wait_recv()
            for k in (1, 2, 3):

                @pl.when(y + k >= NY)
                def _(copy=far[3 * n + k - 1]):
                    copy.start()

    def passed_some(passed, b):
        for copy in passed[1][3 * b : 3 * b + 3]:
            copy.wait_recv()

    row = lax.broadcasted_iota(jnp.int32, (PAIR, PAIR), 0)
    col = lax.broadcasted_iota(jnp.int32, (PAIR, PAIR), 1)
    nt = (((1,), (1,)), ((), ()))

    project(0)
    passed = pass_on(0)

    position = chip * PAIR + lax.broadcasted_iota(jnp.int32, (1, PAIR), 1)
    end = jnp.int32(0)
    start = jnp.zeros((1, PAIR), jnp.int32)
    for n in range(lengths_ref.shape[1]):
        end = end + lengths_ref[0, n]
        start = jnp.where(position >= end, end, start)
    for s in range(4):
        base = chip * PAIR + row
        if s < 3:
            key = base - (3 - s) * PAIR
        else:
            key = jnp.where(row <= col, base, base - 4 * PAIR)
        bias[s] = jnp.where(key >= start, 0.0, -1e30)

    pass_far(passed)
    round_z(4)
    for copy in loads[3:]:
        copy.wait()
    swapq.wait_recv()
    swapg.wait_recv()
    passed_some(passed, 0)

    def prepare(a):
        kt[...] = kv[2 * a].reshape(5 * PAIR, HEAD_SIZE).T
        dkt[...] = jnp.zeros_like(dkt)
        dvt[...] = jnp.zeros_like(dvt)

    upper = jnp.concatenate([row <= col] * TOGETHER, axis=1)

    def attend(a, step, passed=None, leave=None):
        columns = [
            pl.ds(
                pl.multiple_of((a * GROUP + step * TOGETHER + n) * HEAD_SIZE, HEAD_SIZE),
                HEAD_SIZE,
            )
            for n in range(TOGETHER)
        ]
        q = jnp.concatenate([qh[:, c] for c in columns], axis=0)
        g = jnp.concatenate([gh[:, c] for c in columns], axis=0)
        gt = g.T
        keys = kv[2 * a].reshape(5 * PAIR, HEAD_SIZE)

        def blocks(u, v):
            t = lax.dot_general(u, v, nt, preferred_element_type=F32)
            t = [t[s * PAIR : (s + 1) * PAIR] for s in range(5)]
            return [*t[1:4], jnp.where(upper, t[4], t[0])]

        score = [
            t * (SCALE * LOG2E) + jnp.concatenate([bias[s]] * TOGETHER, axis=1)
            for s, t in enumerate(blocks(keys, q))
        ]
        top = functools.reduce(
            jnp.maximum, [jnp.max(t, axis=0, keepdims=True) for t in score]
        )
        weight = [jnp.exp2(t - top) for t in score]
        total = sum(jnp.sum(t, axis=0, keepdims=True) for t in weight)
        inverse = 1.0 / total

        def split(ref, parts):
            for s in range(3):
                ref[(s + 1) * PAIR : (s + 2) * PAIR] = parts[s].astype(BF16)
            ref[0:PAIR] = jnp.where(upper, 0.0, parts[3]).astype(BF16)
            ref[4 * PAIR : 5 * PAIR] = jnp.where(upper, parts[3], 0.0).astype(BF16)

        split(prob_ref, weight)
        if passed is not None:
            passed_some(passed, 1)
            vt[...] = kv[2 * a + 1].reshape(5 * PAIR, HEAD_SIZE).T
        mixed = jnp.dot(vt[...], prob_ref[...], preferred_element_type=F32)
        out = (mixed * inverse).astype(BF16).astype(F32)
        for n, c in enumerate(columns):
            atts[:, c] = out[:, n * PAIR : (n + 1) * PAIR].T.astype(BF16)
        product = jnp.sum(gt.astype(F32) * out, axis=0, keepdims=True)
        prob = [t * inverse for t in weight]
        split(prob_ref, prob)
        dvt[...] += lax.dot_general(gt, prob_ref[...], nt, preferred_element_type=F32)
        if leave is not None:
            leave(a, 1)
        values = kv[2 * a + 1].reshape(5 * PAIR, HEAD_SIZE)
        split(slope_ref, [t * (r - product) for t, r in zip(prob, blocks(values, g))])
        dq = jnp.dot(kt[...], slope_ref[...], preferred_element_type=F32) * SCALE
        for n, c in enumerate(columns):
            dqs[:, c] = dq[:, n * PAIR : (n + 1) * PAIR].T.astype(BF16)
        dkt[...] += lax.dot_general(q.T, slope_ref[...], nt, preferred_element_type=F32)

    def attend_two(a, first):
        lax.fori_loop(first, first + 2, lambda n, c: (attend(a, n), c)[1], 0)

    outs, keeps = [], []
    returns = {}

    def leave(a, b):
        p = 2 * a + b
        part[p] = (dvt[...] if b else dkt[...] * SCALE).T.reshape(5, PAIR, HEAD_SIZE)
        for k in (1, 2, 3):
            stage[p, k] = part[p, 4 - k].astype(BF16)
            returns[p, k] = go(sends.make(stage.at[p, k], land.at[p, k], at("y", -k)))

    def finish(a):
        leave(a, 0)
        cols = pl.ds(a * HALF // 2, HALF // 2)
        for src, ref in ((atts, att_ref), (dqs, dq_ref)):
            place_cols = pl.ds(pl.multiple_of(core * HALF + a * HALF // 2, HALF // 2), HALF // 2)
            outs.append(go(sends.make(src.at[yours, cols], ref.at[:, place_cols], partner)))
            keeps.append(local(src.at[mine, cols], ref.at[:, place_cols]))

    def collect(a):
        ups = {}
        for b in (1, 0):
            p = 2 * a + b
            before, own = part[p, 0], part[p, 4]
            for k in (1, 2, 3):
                returns[p, k].wait_recv()
                value = land[p, k].astype(F32)
                before = before + jnp.where(y + k >= NY, value, 0.0)
                own = own + jnp.where(y + k < NY, value, 0.0)
            stage[p, 0] = before.astype(BF16)
            part[p, 4] = own
            ups[b] = go(sends.make(stage.at[p, 0], land.at[p, 0], at("x", -1)))
        return ups

    def settle(a, ups):
        crosses = []
        for b in (1, 0):
            p = 2 * a + b
            ups[b].wait_recv()
            cols = pl.ds(b * 128, 128)
            block = flat.at[core * 2 + a, :, cols]
            block[...] = (part[p, 4] + land[p, 0].astype(F32)).astype(BF16)
            crosses.append(go(sends.make(block, block, partner)))
        return crosses

    def multiply(a, n, side):
        right = wbuf[a, core * 4 + n] if side is core else wother[a, n]
        return lax.dot_general(
            flat[side * 2 + a], right.reshape(512, 256), nt, preferred_element_type=F32
        )

    prepare(0)
    attend(0, 0, passed)
    for copy in ring[-1]:
        copy.wait_recv()
    project(1)
    passed1 = pass_on(1)
    attend(0, 1)
    attend(0, 2)
    pass_far(passed1)
    attend(0, 3, None, leave)
    finish(0)
    passed_some(passed1, 0)
    prepare(1)
    attend(1, 0, passed1)
    attend(1, 1)
    ups0 = collect(0)
    attend(1, 2)
    crosses0 = settle(0, ups0)
    attend(1, 3, None, leave)
    for copy in crosses0:
        copy.wait_recv()
    passed[3].wait_recv()
    finish(1)
    passed1[3].wait_recv()
    for n in range(4):
        acc[:, n * 512 : (n + 1) * 512] = multiply(0, n, core) + multiply(0, n, other)
    ups1 = collect(1)
    crosses1 = settle(1, ups1)
    for n in range(4):
        acc[:, n * 512 : (n + 1) * 512] += multiply(1, n, core)
    for copy in crosses1:
        copy.wait_recv()
    for n in range(4):
        cols = pl.ds(n * 512, 512)
        placed = pl.ds(pl.multiple_of(core * HALF + n * 512, 512), 512)
        igs[:, cols] = (acc[:, cols] + multiply(1, n, other)).astype(BF16)
        outs.append(go(sends.make(igs.at[yours, cols], ig_ref.at[:, placed], partner)))
        keeps.append(local(igs.at[mine, cols], ig_ref.at[:, placed]))
    for copy in outs:
        copy.wait_recv()
    for copy in started:
        copy.wait_send()
    for copy in keeps:
        copy.wait()


def shards(queries, layer_input, key_value_weight, output_gradient, document_lengths):
    anywhere = pl.BlockSpec(memory_space=pl.ANY)
    shape = jax.ShapeDtypeStruct((TOKENS, MODEL), BF16)
    sems = pltpu.SemaphoreType.DMA
    window = 5 * PAIR
    wide = TOGETHER * PAIR
    att, dq, ig = pl.pallas_call(
        layer_kernel,
        out_shape=(shape,) * 3,
        in_specs=[
            pl.BlockSpec(memory_space=pltpu.SMEM),
            anywhere,
            anywhere,
            anywhere,
            pl.BlockSpec(memory_space=pltpu.VMEM),
        ],
        out_specs=[anywhere] * 3,
        scratch_shapes=[
            pltpu.VMEM((2, NZ, NX, NY, 32, 256), BF16),
            pltpu.VMEM((2, NZ // 2, NX, NY, 32, 256), BF16),
            pltpu.VMEM((PAIR, MODEL), BF16),
            pltpu.VMEM((TOKENS, HALF), BF16),
            pltpu.VMEM((TOKENS, HALF), BF16),
            pltpu.VMEM((PAIR, HALF), BF16),
            pltpu.VMEM((PAIR, HALF), BF16),
            pltpu.VMEM((4, 5, PAIR, HEAD_SIZE), BF16),
            pltpu.VMEM((4, PAIR, PAIR), F32),
            pltpu.VMEM((HEAD_SIZE, window), BF16),
            pltpu.VMEM((HEAD_SIZE, window), BF16),
            pltpu.VMEM((HEAD_SIZE, window), F32),
            pltpu.VMEM((HEAD_SIZE, window), F32),
            pltpu.VMEM((window, wide), BF16),
            pltpu.VMEM((window, wide), BF16),
            pltpu.VMEM((4, 5, PAIR, HEAD_SIZE), F32),
            pltpu.VMEM((4, 4, PAIR, HEAD_SIZE), BF16),
            pltpu.VMEM((4, 4, PAIR, HEAD_SIZE), BF16),
            pltpu.VMEM((4, PAIR, 256), BF16),
            pltpu.VMEM((PAIR, HALF), F32),
            pltpu.VMEM((PAIR, HALF), BF16),
            pltpu.VMEM((PAIR, HALF), BF16),
            pltpu.VMEM((PAIR, HALF), BF16),
            sems((160,)),
            sems((160,)),
            sems((24,)),
        ],
        compiler_params=pltpu.CompilerParams(
            collective_id=0, has_side_effects=True, vmem_limit_bytes=50 << 20
        ),
        name="layer",
    )(document_lengths, queries[0], output_gradient[0], layer_input[0], key_value_weight)
    return (att[None], dq[None], ig[None])


def solution(mesh):
    return jax.shard_map(
        shards,
        mesh=mesh,
        in_specs=(
            P("dp", "ctx", None),
            P("dp", "ctx", None),
            P(("dp", "ctx"), None),
            P("dp", "ctx", None),
            P("dp", None),
        ),
        out_specs=(P("dp", "ctx", None), P("dp", "ctx", None), P("dp", "ctx", None)),
        check_vma=False,
    )
```
